128 devices in a mesh: seq: 64 (over y, z, x), ch: 2 (over core).
Axes of the slice: x: 4, y: 4, z: 4, core: 2. Of those that a mesh axis runs over, the one named last changes fastest.
Arguments:
- cotangent: bfloat16 [16384, 2, 2048], P('seq', None, 'ch'), may hold values from -6 to 6
- conv_input: bfloat16 [16384, 2, 2048], P('seq', None, 'ch'), may hold values from -6 to 6
- decay_rate: bfloat16 [16384, 2048], P('seq', 'ch'), may hold values from 2.4414063e-06 to 0.7
- angle: float32 [2048], P('ch'), may hold values from -3.140625 to 3.140625
- conv_weight: float32 [4, 2, 2048], P(None, None, 'ch'), may hold values from -3 to 3
- in_weight: bfloat16 [4096, 2, 2048], P(None, None, 'ch'), may hold values from -0.09375 to 0.09375
Outputs:
- input_grad: bfloat16 [16384, 4096], P(('seq', 'ch'))
- channel_major: bfloat16 [2, 2048, 16384], P(None, ('ch', 'seq'))
- tap_grad: float32 [4, 2, 2048], P(None, None, 'ch')
The draws below stay inside these ranges and needn't reach their ends.
All inputs are finite; a program needn't handle non-finite values.
Results may differ from the reference program's by a relative error of at most 0.0085.
Values may be sent and summed in bfloat16 or wider, within the bound.
A program may use at most 128 MiB of HBM per device.

```python
import jax
import jax.numpy as jnp
from jax import lax

D = 4096
COMPLEX_CHANNELS = 2048
TOK_DEV = 256
TOKEN_POSITIONS = 16384
N_SEQ = 64
N_CH = 2


def draw_decay_rate(key, part):
    random_subkey_list = jax.random.split(key, 7)
    slow_share = 0.5
    picker = jax.random.uniform(random_subkey_list[0], (COMPLEX_CHANNELS,))
    slow_mask = picker < slow_share
    base_slow = jnp.exp(jax.random.uniform(random_subkey_list[1], (COMPLEX_CHANNELS,), minval=jnp.log(0.2 / TOKEN_POSITIONS), maxval=jnp.log(0.6 / TOKEN_POSITIONS)))
    base_fast = jnp.exp(jax.random.uniform(random_subkey_list[2], (COMPLEX_CHANNELS,), minval=jnp.log(1.0 / 50.0), maxval=jnp.log(1.0 / 30.0)))
    baseline_rate = jnp.where(slow_mask, base_slow, base_fast)
    jitter_amount = jax.random.uniform(random_subkey_list[3], (TOKEN_POSITIONS, COMPLEX_CHANNELS), minval=0.5, maxval=1.5)
    phase_shift = jax.random.uniform(random_subkey_list[4], (COMPLEX_CHANNELS,), minval=0.0, maxval=6.2831853)
    position = jnp.arange(TOKEN_POSITIONS, dtype=jnp.float32) / TOKEN_POSITIONS
    rate_envelope = jnp.exp(0.7 * jnp.sin(6.2831853 * 3.0 * position[:, None] + phase_shift[None, :]))
    spike_locations = jax.random.randint(random_subkey_list[5], (2,), 0, TOKEN_POSITIONS)
    spike_rows = jnp.any(jnp.arange(TOKEN_POSITIONS)[:, None] == spike_locations[None, :], axis=1)
    spike_rate = jax.random.uniform(random_subkey_list[6], (COMPLEX_CHANNELS,), minval=0.22, maxval=0.51)
    combined_rate = baseline_rate[None, :] * jitter_amount * rate_envelope + jnp.where(spike_rows[:, None], spike_rate[None, :], 0.0)
    return combined_rate.astype(jnp.float32).astype(jnp.bfloat16)


def level_of(key, dims, shards, least, largest):
    def one(axis_at, blocks):
        heights = jax.random.uniform(jax.random.fold_in(jax.random.fold_in(key, 6), axis_at), (blocks,), jnp.float32, least / len(shards), largest / len(shards))
        return jnp.repeat(jnp.exp(heights), dims[axis_at] // blocks).reshape((-1,) + (1,) * (len(dims) - axis_at - 1))

    loudness = one(*shards[0])
    for cut in shards[1:]:
        loudness = loudness * one(*cut)
    return loudness


def centred(rng, shape, spread, reach, cuts=(), kind=jnp.bfloat16):
    entries = jax.random.normal(rng, shape, jnp.float32) * spread
    if len(cuts) > 0:
        entries = level_of(rng, shape, cuts, -0.22, 0.18) * entries
    return jnp.clip(entries, min=-reach, max=reach).astype(kind)


def setup_inputs(seed: int = 0) -> dict:
    arg_keys = jax.random.split(jax.random.key(seed), 7)
    cotangent = centred(arg_keys[0], (TOKEN_POSITIONS, 2, COMPLEX_CHANNELS), 1.0, 6.0, ((0, 64), (2, 2)))
    conv_input = centred(arg_keys[1], (TOKEN_POSITIONS, 2, COMPLEX_CHANNELS), 1.0, 6.0, ((0, 64), (2, 2)))
    decay_rate = draw_decay_rate(jax.random.fold_in(arg_keys[6], 71), 0)
    angle = jnp.clip(jax.random.uniform(arg_keys[3], (COMPLEX_CHANNELS,), jnp.float32, -3.140625, 3.140625), -3.140625, 3.140625)
    conv_weight = centred(arg_keys[4], (4, 2, COMPLEX_CHANNELS), 4 ** -0.5, 3.0, ((2, 2),), jnp.float32)
    in_weight = centred(arg_keys[5], (D, 2, COMPLEX_CHANNELS), (2 * COMPLEX_CHANNELS) ** -0.5, 0.09375, ((2, 2),))
    return dict(cotangent=cotangent, conv_input=conv_input, decay_rate=decay_rate, angle=angle, conv_weight=conv_weight, in_weight=in_weight)


def compose(earlier, later):
    outer_real, outer_imag, outer_shift_real, outer_shift_imag = earlier
    inner_real, inner_imag, inner_shift_real, inner_shift_imag = later
    return (inner_real * outer_real - inner_imag * outer_imag, inner_real * outer_imag + inner_imag * outer_real, inner_real * outer_shift_real - inner_imag * outer_shift_imag + inner_shift_real, inner_real * outer_shift_imag + inner_imag * outer_shift_real + inner_shift_imag)

def local_block(cotangent, decay_rate, angle):
    rates = decay_rate.astype(jnp.float32)
    modulus = jnp.exp(-rates)
    mult_real = modulus * jnp.cos(angle)[None, :]
    mult_imag = -modulus * jnp.sin(angle)[None, :]
    step_real = jnp.concatenate([mult_real[1:], jnp.ones_like(mult_real[:1])], 0)
    step_imag = jnp.concatenate([mult_imag[1:], jnp.zeros_like(mult_imag[:1])], 0)
    upstream = cotangent.astype(jnp.float32)
    elements = (step_real[::-1], step_imag[::-1], upstream[::-1, 0], upstream[::-1, 1])
    scanned = lax.associative_scan(compose, elements, axis=0)
    prod_real, prod_imag, base_real, base_imag = [member[::-1] for member in scanned]
    return (mult_real, mult_imag, prod_real, prod_imag, base_real, base_imag)

def reference(cotangent, conv_input, decay_rate, angle, conv_weight, in_weight):
    blocks_cot = cotangent.reshape(N_SEQ, TOK_DEV, 2, COMPLEX_CHANNELS)
    blocks_rate = decay_rate.reshape(N_SEQ, TOK_DEV, COMPLEX_CHANNELS)

    def sweep(carry, inputs):
        carry_real, carry_imag = carry
        cot_block, rate_block = inputs
        mult_real, mult_imag, prod_real, prod_imag, base_real, base_imag = local_block(cot_block, rate_block, angle)
        grad_real = base_real + prod_real * carry_real[None] - prod_imag * carry_imag[None]
        grad_imag = base_imag + prod_real * carry_imag[None] + prod_imag * carry_real[None]
        next_real = mult_real[0] * grad_real[0] - mult_imag[0] * grad_imag[0]
        next_imag = mult_real[0] * grad_imag[0] + mult_imag[0] * grad_real[0]
        return ((next_real, next_imag), jnp.stack([grad_real, grad_imag], 1))
    zero_state = jnp.zeros((COMPLEX_CHANNELS,), jnp.float32)
    final_carry, grads = lax.scan(sweep, (zero_state, zero_state), (blocks_cot, blocks_rate), reverse=True)
    state_grad = grads.reshape(TOKEN_POSITIONS, 2, COMPLEX_CHANNELS)
    rates = decay_rate.astype(jnp.float32)
    scaling = jnp.sqrt(-jnp.expm1(-2.0 * rates))
    conv_grad = state_grad * scaling[:, None, :]
    tail_zeros = jnp.zeros((3, 2, COMPLEX_CHANNELS), jnp.float32)
    extended = jnp.concatenate([conv_grad, tail_zeros], 0)
    feature_sum = conv_weight[0][None] * extended[0:TOKEN_POSITIONS]
    for tap_index in range(1, 4):
        feature_sum = feature_sum + conv_weight[tap_index][None] * extended[tap_index:tap_index + TOKEN_POSITIONS]
    input_feat = feature_sum.astype(jnp.bfloat16)
    shifted_input = jnp.concatenate([tail_zeros, conv_input.astype(jnp.float32)], 0)
    taps = []
    for tap_index in range(4):
        taps.append(lax.optimization_barrier(jnp.sum(conv_grad * shifted_input[3 - tap_index:3 - tap_index + TOKEN_POSITIONS], axis=0)))
    tap_grad = jnp.stack(taps, 0)
    block_width = COMPLEX_CHANNELS // N_CH
    feat_blocks = input_feat.reshape(TOKEN_POSITIONS, 2, N_CH, block_width)
    weight_blocks = in_weight.reshape(D, 2, N_CH, block_width)
    total = jnp.zeros((TOKEN_POSITIONS, D), jnp.float32)
    for block_index in range(N_CH):
        left = feat_blocks[:, :, block_index].reshape(TOKEN_POSITIONS, 2 * block_width)
        right = weight_blocks[:, :, block_index].reshape(D, 2 * block_width)
        partial_sum = jnp.dot(left, right.T, preferred_element_type=jnp.float32)
        total = total + partial_sum.astype(jnp.bfloat16).astype(jnp.float32)
    input_grad = total.astype(jnp.bfloat16)
    channel_major = jnp.transpose(input_feat, (1, 2, 0))
    return (input_grad, channel_major, tap_grad)
```

```python
import functools

import jax
import jax.numpy as jnp
from jax import lax
from jax.experimental import pallas as pl
from jax.experimental.pallas import tpu as pltpu
from jax.sharding import PartitionSpec as P

MESH = pl.DeviceIdType.MESH
F32 = jnp.float32
BF16 = jnp.bfloat16
CHUNKS = 8
WCH = 8
EARLY = 8
NT = 8


def cmul(ar, ai, br, bi):
    return ar * br - ai * bi, ar * bi + ai * br


def kernel(
    n_seq, T, C, D,
    cot_h, x_h, dec_h, ang_ref, cw_ref, w_h,
    out_h, cm_h, tap_ref,
    cot_b, x_b, dec_b, w_b, halo_c, halo_d,
    cot_f, x_f, dec_f, e_f, g_f, wtmp, wk, ftmp, feat, featT,
    mapv, maps, part, part_r, obuf, tbuf, trcv, trow,
    in_sem, w_sem, halo_s, halo_r, map_s, map_r, a2a_s, a2a_r, loc_s, par_s, par_r, t1_s, t1_r, t2_s, t2_r, o_sem,
):
    me = lax.axis_index("seq")
    ch = lax.axis_index("ch")
    other = 1 - ch
    NJ = C // 128
    L = T // CHUNKS

    def peer(s):
        return lax.rem(me + s, n_seq)

    barrier = pltpu.get_barrier_semaphore()

    def greet(s, _):
        pl.semaphore_signal(barrier, inc=1, device_id=(peer(s), ch), device_id_type=MESH)
        return 0

    lax.fori_loop(1, n_seq, greet, 0)
    pl.semaphore_signal(barrier, inc=1, device_id=(me, other), device_id_type=MESH)

    c_dec = pltpu.make_async_copy(dec_h, dec_b, in_sem.at[0])
    c_cot = pltpu.make_async_copy(cot_h, cot_b, in_sem.at[1])
    c_x = pltpu.make_async_copy(x_h, x_b, in_sem.at[2])
    c_dec.start()
    c_cot.start()
    c_x.start()
    wrows = w_h.shape[0] // WCH
    for i in range(WCH):
        pltpu.make_async_copy(
            w_h.at[pl.ds(i * wrows, wrows)], w_b.at[pl.ds(i * wrows, wrows)], w_sem.at[i]
        ).start()

    ang = ang_ref[...]
    cr = jnp.cos(ang)
    ci = -jnp.sin(ang)

    def to_f32(src, dst):
        def body(i, _):
            r = pl.multiple_of(i * 64, 64)
            dst[pl.ds(r, 64), :] = src[pl.ds(r, 64), :].astype(F32)
            return 0

        lax.fori_loop(0, src.shape[0] // 64, body, 0)

    def pair(ref, t):
        return ref[pl.ds(2 * NJ * t, NJ, stride=2), :], ref[pl.ds(2 * NJ * t + 1, NJ, stride=2), :]

    c_dec.wait()
    to_f32(dec_b, dec_f)
    c_cot.wait()
    to_f32(cot_b, cot_f)

    zero = jnp.zeros((NJ, 128), F32)

    def pass1(n, st):
        j = L - 1 - n
        out = []
        for c in range(CHUNKS):
            ur, ui, rs = st[3 * c : 3 * c + 3]
            t = c * L + j
            r = dec_f[pl.ds(8 * NJ * (t // 8) + lax.rem(t, 8), NJ, stride=8), :]
            e = jnp.exp(-r)
            e_f[t] = e
            a, b = pair(cot_f, t)
            ur, ui = cmul(e * cr, e * ci, a + ur, b + ui)
            out += [ur, ui, rs + r]
        return tuple(out)

    st = lax.fori_loop(0, L, pass1, (zero,) * (3 * CHUNKS))

    def power(n):
        ar, ai = cr, ci
        while n > 1:
            ar, ai = ar * ar - ai * ai, 2.0 * ar * ai
            n //= 2
        return ar, ai

    lr, li = power(L)
    tr, ti = power(T)
    chunk_maps = []
    for c in range(CHUNKS):
        ur, ui, rs = st[3 * c : 3 * c + 3]
        p = jnp.exp(-rs)
        chunk_maps.append((p * lr, p * li, ur, ui))
    br, bi = zero, zero
    total = zero
    for c in reversed(range(CHUNKS)):
        ar, ai, sr, si = chunk_maps[c]
        br, bi = cmul(ar, ai, br, bi)
        br, bi = br + sr, bi + si
        total = total + st[3 * c + 2]
    mapv[0] = jnp.exp(-total)
    mapv[1] = br
    mapv[2] = bi

    pl.semaphore_wait(barrier, n_seq)

    def map_copy(src_dev, dst_dev):
        return pltpu.make_async_remote_copy(
            src_ref=mapv, dst_ref=maps.at[src_dev], send_sem=map_s.at[dst_dev], recv_sem=map_r.at[src_dev],
            device_id=(dst_dev, ch), device_id_type=MESH)

    def halo_copies(dst_dev):
        return [
            pltpu.make_async_remote_copy(
                src_ref=s, dst_ref=d, send_sem=halo_s.at[i], recv_sem=halo_r.at[i],
                device_id=(dst_dev, ch), device_id_type=MESH)
            for i, (s, d) in enumerate(
                ((cot_b.at[pl.ds(0, 64)], halo_c), (dec_b.at[pl.ds(0, 64)], halo_d)))
        ]

    def send_map(s, _):
        map_copy(me, me - 1 - s).start()
        return 0

    lax.fori_loop(0, me, send_map, 0)

    @pl.when(me > 0)
    def _():
        for c in halo_copies(me - 1):
            c.start()

    def scale_body(t, _):
        r = dec_f[pl.ds(8 * NJ * (t // 8) + lax.rem(t, 8), NJ, stride=8), :]
        g_f[t, 0] = scale_of(r)
        return 0

    def scale_of(r):
        y = 0.25 * r
        q = y * (1.0 - y * (1 / 2) * (1.0 - y * (1 / 3) * (1.0 - y * (1 / 4) * (1.0 - y * (1 / 5) * (1.0 - y * (1 / 6))))))
        q = q * (2.0 - q)
        q = q * (2.0 - q)
        q = q * (2.0 - q)
        return jnp.sqrt(q)

    lax.fori_loop(0, T, scale_body, 0)
    c_x.wait()
    to_f32(x_b, x_f)

    def w_wait(i):
        pltpu.make_async_copy(
            w_h.at[pl.ds(i * wrows, wrows)], w_b.at[pl.ds(i * wrows, wrows)], w_sem.at[i]
        ).wait()

    G = 16 * 2 * NJ

    def unpack_w(i):
        w_wait(i)
        base = i * (wrows // (2 * NJ))

        def body(k, _):
            d0 = pl.multiple_of(base + k * 16, 16)
            slot = lax.rem(k, 2)
            tmp = wtmp.at[slot]
            tmp[...] = w_b[pl.ds(pl.multiple_of(d0 * 2 * NJ, G), G), :].astype(F32)
            for p in range(2):
                for jt in range(NJ):
                    v = tmp[pl.ds(2 * jt + p, 16, stride=2 * NJ), :]
                    wk[pl.ds(d0, 16), pl.ds(p * C + jt * 128, 128)] = v.astype(BF16)
            return 0

        lax.fori_loop(0, wrows // G, body, 0)

    for i in range(EARLY):
        unpack_w(i)

    def compose(n, u):
        j = n_seq - 1 - n
        map_copy(j, me).wait_recv()
        p = maps[j, 0]
        vr, vi = cmul(p * tr, p * ti, u[0], u[1])
        return vr + maps[j, 1], vi + maps[j, 2]

    ur, ui = lax.fori_loop(0, n_seq - 1 - me, compose, (zero, zero))

    last = me == n_seq - 1

    @pl.when(jnp.logical_not(last))
    def _():
        for c in halo_copies(0):
            c.wait_recv()
        hc = halo_c[...].astype(F32)
        hd = halo_d[...].astype(F32)
        ftmp[0, pl.ds(0, 64), :] = hc
        ftmp[1, pl.ds(0, 64), :] = hd
        vr, vi = ur, ui
        for t in range(3):
            r = ftmp[1, pl.ds(t, NJ, stride=8), :]
            e = jnp.exp(r)
            vr, vi = cmul(e * cr, -e * ci, vr, vi)
            s = scale_of(r)
            g_f[T + t, 0] = s * vr
            g_f[T + t, 1] = s * vi
            a, b = ftmp[0, pl.ds(2 * NJ * t, NJ, stride=2), :], ftmp[0, pl.ds(2 * NJ * t + 1, NJ, stride=2), :]
            vr, vi = vr - a, vi - b

    @pl.when(last)
    def _():
        for t in range(3):
            g_f[T + t, 0] = zero
            g_f[T + t, 1] = zero

    init = [None] * CHUNKS
    for c in reversed(range(CHUNKS)):
        init[c] = (ur, ui)
        ar, ai, sr, si = chunk_maps[c]
        ur, ui = cmul(ar, ai, ur, ui)
        ur, ui = ur + sr, ui + si

    def pass2(n, st):
        j = L - 1 - n
        out = []
        for c in range(CHUNKS):
            ur, ui = st[2 * c : 2 * c + 2]
            t = c * L + j
            a, b = pair(cot_f, t)
            a, b = a + ur, b + ui
            s = g_f[t, 0]
            g_f[t, 0] = s * a
            g_f[t, 1] = s * b
            e = e_f[t]
            out += list(cmul(e * cr, e * ci, a, b))
        return tuple(out)

    lax.fori_loop(0, L, pass2, tuple(v for u in init for v in u))

    cw = [[cw_ref[pl.ds(2 * NJ * k + p, NJ, stride=2), :] for p in range(2)] for k in range(4)]

    def conv(i, _):
        for p in range(2):
            g = [g_f[i * 16 + k, p] for k in range(3)]
            for u in range(16):
                g.append(g_f[i * 16 + u + 3, p])
                f = cw[0][p] * g[u] + cw[1][p] * g[u + 1] + cw[2][p] * g[u + 2] + cw[3][p] * g[u + 3]
                ftmp[p, pl.ds((u // 8) * 8 * NJ + u % 8, NJ, stride=8), :] = f
            for jt in range(NJ):
                v = jnp.concatenate([ftmp[p, pl.ds(jt * 8, 8), :], ftmp[p, pl.ds(8 * NJ + jt * 8, 8), :]], 0)
                feat[pl.ds(pl.multiple_of(i * 16, 16), 16), pl.ds(p * C + jt * 128, 128)] = v.astype(BF16)
        return 0

    lax.fori_loop(0, T // 16, conv, 0)

    own = C // n_seq
    per = 128 // own

    def a2a_copy(src_dev, dst_dev):
        return pltpu.make_async_remote_copy(
            src_ref=featT.at[:, pl.ds(pl.multiple_of(dst_dev * own, own), own), :],
            dst_ref=cm_h.at[:, :, pl.ds(pl.multiple_of(src_dev * T, T), T)],
            send_sem=a2a_s.at[dst_dev], recv_sem=a2a_r.at[src_dev],
            device_id=(dst_dev, ch), device_id_type=MESH)

    local = pltpu.make_async_copy(
        featT.at[:, pl.ds(pl.multiple_of(me * own, own), own), :],
        cm_h.at[:, :, pl.ds(pl.multiple_of(me * T, T), T)], loc_s)

    def turn(s, _):
        jt = lax.rem(me // per + s, NJ)
        for p in range(2):
            blk = feat[:, pl.ds(pl.multiple_of(p * C + jt * 128, 128), 128)]
            featT[p, pl.ds(pl.multiple_of(jt * 128, 128), 128), :] = blk.T

        def send(q, _):
            j = jt * per + lax.rem(me + q, per)

            @pl.when(j != me)
            def _():
                a2a_copy(me, j).start()

            @pl.when(j == me)
            def _():
                local.start()

            return 0

        lax.fori_loop(0, per, send, 0)
        return 0

    lax.fori_loop(0, NJ, turn, 0)

    def taps(i, acc):
        acc = list(acc)
        for p in range(2):
            g = [g_f[i * 4 + k, p] for k in range(3)]
            for u in range(4):
                g.append(g_f[i * 4 + u + 3, p])
                x = x_f[pl.ds(2 * NJ * (i * 4 + u) + p, NJ, stride=2), :]
                for k in range(4):
                    acc[2 * k + p] = acc[2 * k + p] + g[u + k] * x
        return tuple(acc)

    acc = lax.fori_loop(0, T // 4, taps, (zero,) * 8)
    for k in range(4):
        for p in range(2):
            for jt in range(NJ):
                tbuf[2 * NJ * k + 2 * jt + p] = acc[2 * k + p][jt : jt + 1, :]
    trcv[me] = tbuf[me]

    def t1(src_dev, dst_dev):
        return pltpu.make_async_remote_copy(
            src_ref=tbuf.at[dst_dev], dst_ref=trcv.at[src_dev], send_sem=t1_s.at[dst_dev], recv_sem=t1_r.at[src_dev],
            device_id=(dst_dev, ch), device_id_type=MESH)

    def t2(src_dev, dst_dev):
        return pltpu.make_async_remote_copy(
            src_ref=trow, dst_ref=tap_ref.at[src_dev], send_sem=t2_s.at[dst_dev], recv_sem=t2_r.at[src_dev],
            device_id=(dst_dev, ch), device_id_type=MESH)

    def others(fn):
        def body(s, _):
            fn(peer(s))
            return 0

        lax.fori_loop(1, n_seq, body, 0)

    others(lambda j: t1(me, j).start())

    for i in range(EARLY, WCH):
        unpack_w(i)

    nt = D // NT
    half = T // 2

    def par_copy(n):
        cols = pl.ds(pl.multiple_of(n * nt, nt), nt)
        return pltpu.make_async_remote_copy(
            src_ref=part.at[pl.ds(pl.multiple_of(other * half, half), half), cols], dst_ref=part_r.at[:, cols],
            send_sem=par_s.at[n], recv_sem=par_r.at[n], device_id=(me, other), device_id_type=MESH)

    def tile(n, _):
        rows = pl.ds(pl.multiple_of(n * nt, nt), nt)
        y = lax.dot_general(feat[...], wk[rows, :], (((1,), (1,)), ((), ())), preferred_element_type=F32)
        part[:, rows] = y.astype(BF16)
        par_copy(n).start()
        return 0

    lax.fori_loop(0, NT, tile, 0)

    others(lambda j: t1(j, me).wait_recv())
    row = jnp.sum(trcv[...], axis=0)
    trow[...] = row
    tap_ref[me] = row
    others(lambda j: t2(me, j).start())

    def out_copy(n):
        cols = pl.ds(pl.multiple_of(n * nt, nt), nt)
        return pltpu.make_async_copy(obuf.at[:, cols], out_h.at[:, cols], o_sem.at[n])

    def join(n, _):
        par_copy(n).wait_recv()
        cols = pl.ds(pl.multiple_of(n * nt, nt), nt)
        mine = part[pl.ds(pl.multiple_of(ch * half, half), half), cols]
        obuf[:, cols] = (mine.astype(F32) + part_r[:, cols].astype(F32)).astype(BF16)
        out_copy(n).start()
        return 0

    lax.fori_loop(0, NT, join, 0)

    def sent(s, _):
        map_copy(me, me - 1 - s).wait_send()
        return 0

    lax.fori_loop(0, me, sent, 0)

    @pl.when(me > 0)
    def _():
        for c in halo_copies(me - 1):
            c.wait_send()

    def ends(n, _):
        par_copy(n).wait_send()
        out_copy(n).wait()
        return 0

    lax.fori_loop(0, NT, ends, 0)

    def drain(j):
        t1(me, j).wait_send()
        t2(me, j).wait_send()
        a2a_copy(me, j).wait_send()
        t2(j, me).wait_recv()
        a2a_copy(j, me).wait_recv()

    others(drain)
    local.wait()


def solution(mesh):
    n_seq = mesh.shape["seq"]

    def flat(a):
        lead = a.shape[0]
        return a.reshape(lead, 2, -1, 128).transpose(0, 2, 1, 3).reshape(-1, 128)

    def on_device(cotangent, conv_input, decay_rate, angle, conv_weight, in_weight):
        T, _, C = cotangent.shape
        D = in_weight.shape[0]
        NJ = C // 128
        dec = decay_rate.reshape(T // 8, 8, NJ, 128).transpose(0, 2, 1, 3).reshape(-1, 128)
        dma = pltpu.SemaphoreType.DMA
        ANY = pl.BlockSpec(memory_space=pl.ANY)
        V = pl.BlockSpec(memory_space=pltpu.VMEM)
        rows = 8 * NJ
        out, cm, tap = pl.pallas_call(
            functools.partial(kernel, n_seq, T, C, D),
            out_shape=(
                jax.ShapeDtypeStruct((T // 2, D), BF16),
                jax.ShapeDtypeStruct((2, C // n_seq, T * n_seq), BF16),
                jax.ShapeDtypeStruct((rows, 1, 128), F32),
            ),
            in_specs=[ANY, ANY, ANY, V, V, ANY],
            out_specs=(ANY, ANY, V),
            scratch_shapes=[
                pltpu.VMEM((T * 2 * NJ, 128), BF16),
                pltpu.VMEM((T * 2 * NJ, 128), BF16),
                pltpu.VMEM((T * NJ, 128), BF16),
                pltpu.VMEM((D * 2 * NJ, 128), BF16),
                pltpu.VMEM((64, 128), BF16),
                pltpu.VMEM((64, 128), BF16),
                pltpu.VMEM((T * 2 * NJ, 128), F32),
                pltpu.VMEM((T * 2 * NJ, 128), F32),
                pltpu.VMEM((T * NJ, 128), F32),
                pltpu.VMEM((T, NJ, 128), F32),
                pltpu.VMEM((T + 3, 2, NJ, 128), F32),
                pltpu.VMEM((2, 32 * NJ, 128), F32),
                pltpu.VMEM((D, 2 * C), BF16),
                pltpu.VMEM((2, 16 * NJ, 128), F32),
                pltpu.VMEM((T, 2 * C), BF16),
                pltpu.VMEM((2, C, T), BF16),
                pltpu.VMEM((3, NJ, 128), F32),
                pltpu.VMEM((n_seq, 3, NJ, 128), F32),
                pltpu.VMEM((T, D), BF16),
                pltpu.VMEM((T // 2, D), BF16),
                pltpu.VMEM((T // 2, D), BF16),
                pltpu.VMEM((rows, 1, 128), F32),
                pltpu.VMEM((n_seq, 1, 128), F32),
                pltpu.VMEM((1, 128), F32),
                dma((3,)), dma((WCH,)), dma((2,)), dma((2,)),
                dma((n_seq,)), dma((n_seq,)), dma((n_seq,)), dma((n_seq,)), dma,
                dma((NT,)), dma((NT,)),
                dma((n_seq,)), dma((n_seq,)), dma((n_seq,)), dma((n_seq,)), dma((NT,)),
            ],
            compiler_params=pltpu.CompilerParams(
                collective_id=0, has_side_effects=True, vmem_limit_bytes=62 * 1024 * 1024),
        )(flat(cotangent), flat(conv_input), dec, angle.reshape(NJ, 128), flat(conv_weight), flat(in_weight))
        tap = tap.reshape(4, NJ, 2, 128).transpose(0, 2, 1, 3).reshape(4, 2, C)
        return out, cm, tap

    in_specs = (
        P("seq", None, "ch"),
        P("seq", None, "ch"),
        P("seq", "ch"),
        P("ch"),
        P(None, None, "ch"),
        P(None, None, "ch"),
    )
    out_specs = (P(("seq", "ch"), None), P(None, ("ch", "seq"), None), P(None, None, "ch"))
    return jax.shard_map(on_device, mesh=mesh, in_specs=in_specs, out_specs=out_specs, check_vma=False)
```

```python
import functools

import jax
import jax.numpy as jnp
from jax import lax
from jax.experimental import pallas as pl
from jax.experimental.pallas import tpu as pltpu
from jax.sharding import PartitionSpec as P

MESH = pl.DeviceIdType.MESH
F32 = jnp.float32
BF16 = jnp.bfloat16
CHUNKS = 8
WCH = 8
W1, W2, W3 = 1, 4, 7
UNR = 2
NT = 8
RING = 4
STAGES = 3


def cmul(ar, ai, br, bi):
    return ar * br - ai * bi, ar * bi + ai * br


def scale_of(r):
    y = 0.25 * r
    q = y * (1.0 - y * (1 / 2) * (1.0 - y * (1 / 3) * (1.0 - y * (1 / 4) * (1.0 - y * (1 / 5) * (1.0 - y * (1 / 6))))))
    q = q * (2.0 - q)
    q = q * (2.0 - q)
    q = q * (2.0 - q)
    return jnp.sqrt(q)


def kernel(
    n_seq, T, C, D,
    cot_h, x_h, dec_h, ang_ref, cw_ref, w_h,
    out_h, cm_h, tap_ref,
    cot_b, x_b, dec_b, w_b, halo_c, halo_d,
    cot_f, x_f, e_f, sc_f, g_f, wtmp, wk, ftmp, feat, featT,
    mapv, maps, part, part_r, obuf, tbuf, trcv, trow,
    in_sem, w_sem, halo_s, halo_r, map_s, map_r, a2a_s, a2a_r, loc_s, par_s, par_r, t1_s, t1_r, t2_s, t2_r, o_sem,
):
    me = lax.axis_index("seq")
    ch = lax.axis_index("ch")
    other = 1 - ch
    NJ = C // 128
    L = T // CHUNKS
    strides = [RING**k for k in range(STAGES)]
    place = [lax.rem(me // st, RING) for st in strides]

    def ring(k, s):
        return me + (lax.rem(place[k] + s, RING) - place[k]) * strides[k]

    barrier = pltpu.get_barrier_semaphore()

    def greet(dev, core):
        pl.semaphore_signal(barrier, inc=1, device_id=(dev, core), device_id_type=MESH)

    for k in range(STAGES):
        for s in range(1, RING):
            greet(ring(k, s), ch)
    before, after = lax.rem(me + n_seq - 1, n_seq), lax.rem(me + 1, n_seq)
    greet(before, ch)
    greet(after, ch)
    greet(me, other)
    greetings = STAGES * (RING - 1) + 3

    c_dec = pltpu.make_async_copy(dec_h, dec_b, in_sem.at[0])
    c_cot = pltpu.make_async_copy(cot_h, cot_b, in_sem.at[1])
    c_x = pltpu.make_async_copy(x_h, x_b, in_sem.at[2])
    c_dec.start()
    c_cot.start()
    c_x.start()
    wrows = w_h.shape[0] // WCH

    def w_copy(i):
        return pltpu.make_async_copy(
            w_h.at[pl.ds(i * wrows, wrows)], w_b.at[pl.ds(i * wrows, wrows)], w_sem.at[i])

    for i in range(WCH):
        w_copy(i).start()

    ang = ang_ref[...]
    cr = jnp.cos(ang)
    ci = -jnp.sin(ang)

    def rowwise(src, dst, fn):
        def body(i, _):
            r = pl.multiple_of(i * 64, 64)
            dst[pl.ds(r, 64), :] = fn(src[pl.ds(r, 64), :].astype(F32))
            return 0

        lax.fori_loop(0, src.shape[0] // 64, body, 0)

    def pair(ref, t):
        return ref[pl.ds(2 * NJ * t, NJ, stride=2), :], ref[pl.ds(2 * NJ * t + 1, NJ, stride=2), :]

    c_dec.wait()
    rowwise(dec_b, e_f, lambda r: jnp.exp(-r))
    c_cot.wait()
    rowwise(cot_b, cot_f, lambda v: v)

    zero = jnp.zeros((NJ, 128), F32)
    one = jnp.ones((NJ, 128), F32)

    def at(t8, u):
        return pl.ds(8 * NJ * t8 + u, NJ, stride=8)

    def pass1(n, st):
        st = list(st)
        for u in reversed(range(8)):
            for c in range(CHUNKS):
                t8 = c * (L // 8) + L // 8 - 1 - n
                ur, ui, p = st[3 * c : 3 * c + 3]
                e = e_f[at(t8, u), :]
                a, b = pair(cot_f, t8 * 8 + u)
                ur, ui = cmul(e * cr, e * ci, a + ur, b + ui)
                st[3 * c : 3 * c + 3] = ur, ui, p * e
        return tuple(st)

    st = lax.fori_loop(0, L // 8, pass1, (zero, zero, one) * CHUNKS)

    def power(ar, ai, n):
        while n > 1:
            ar, ai = ar * ar - ai * ai, 2.0 * ar * ai
            n //= 2
        return ar, ai

    lr, li = power(cr, ci, L)
    rot = power(lr, li, CHUNKS)
    chunk_maps = []
    for c in range(CHUNKS):
        ur, ui, p = st[3 * c : 3 * c + 3]
        chunk_maps.append((p * lr, p * li, ur, ui))
    br, bi = zero, zero
    total = one
    for c in reversed(range(CHUNKS)):
        ar, ai, sr, si = chunk_maps[c]
        br, bi = cmul(ar, ai, br, bi)
        br, bi = br + sr, bi + si
        total = total * st[3 * c + 2]

    pl.semaphore_wait(barrier, greetings)

    def halo_copies(dst_dev):
        return [
            pltpu.make_async_remote_copy(
                src_ref=s, dst_ref=d, send_sem=halo_s.at[i], recv_sem=halo_r.at[i],
                device_id=(dst_dev, ch), device_id_type=MESH)
            for i, (s, d) in enumerate(
                ((cot_b.at[pl.ds(0, 64)], halo_c), (dec_b.at[pl.ds(0, 64)], halo_d)))
        ]

    def map_copy(k, s):
        return pltpu.make_async_remote_copy(
            src_ref=mapv.at[k], dst_ref=maps.at[k, place[k]], send_sem=map_s.at[k, s], recv_sem=map_r.at[k, RING - s],
            device_id=(ring(k, s), ch), device_id_type=MESH)

    def send_map(k, p, br, bi):
        for i, v in enumerate((p, br, bi)):
            mapv[k, i] = v
            maps[k, place[k], i] = v
        for s in range(1, RING):
            map_copy(k, s).start()

    def stage(k, rot):
        for s in range(1, RING):
            map_copy(k, s).wait_recv()
        ar, ai, br, bi, p = one, zero, zero, zero, one
        mine = None
        for j in reversed(range(RING)):
            here = place[k] == j
            now = (ar, ai, br, bi)
            mine = now if mine is None else tuple(jnp.where(here, x, y) for x, y in zip(now, mine))
            q = maps[k, j, 0]
            vr, vi = q * rot[0], q * rot[1]
            br, bi = cmul(vr, vi, br, bi)
            br, bi = br + maps[k, j, 1], bi + maps[k, j, 2]
            if j > 0:
                ar, ai = cmul(vr, vi, ar, ai)
            p = p * q
        return mine, (p, br, bi)

    send_map(0, total, br, bi)

    @pl.when(me > 0)
    def _():
        for c in halo_copies(before):
            c.start()

    G = 16 * 2 * NJ

    def unpack_w(i):
        w_copy(i).wait()
        base = i * (wrows // (2 * NJ))

        def body(k, _):
            for v in range(UNR):
                d0 = pl.multiple_of(base + k * (16 * UNR) + v * 16, 16)
                tmp = wtmp.at[v]
                tmp[...] = w_b[pl.ds(pl.multiple_of(d0 * 2 * NJ, G), G), :].astype(F32)
                for p in range(2):
                    for jt in range(NJ):
                        x = tmp[pl.ds(2 * jt + p, 16, stride=2 * NJ), :]
                        wk[p * NJ + jt, pl.ds(d0, 16), :] = x.astype(BF16)
            return 0

        lax.fori_loop(0, wrows // (G * UNR), body, 0)

    rowwise(dec_b, sc_f, scale_of)
    c_x.wait()
    rowwise(x_b, x_f, lambda v: v)
    for i in range(0, W1):
        unpack_w(i)

    later0, whole0 = stage(0, rot)
    send_map(1, *whole0)
    for i in range(W1, W2):
        unpack_w(i)
    rot1 = power(*rot, RING)
    later1, whole1 = stage(1, rot1)
    send_map(2, *whole1)
    for i in range(W2, W3):
        unpack_w(i)
    later2, _ = stage(2, power(*rot1, RING))

    ur, ui = later2[2], later2[3]
    for ar, ai, br, bi in (later1, later0):
        ur, ui = cmul(ar, ai, ur, ui)
        ur, ui = ur + br, ui + bi

    last = me == n_seq - 1

    @pl.when(jnp.logical_not(last))
    def _():
        for c in halo_copies(before):
            c.wait_recv()
        ftmp[0, pl.ds(0, 64), :] = halo_c[...].astype(F32)
        ftmp[1, pl.ds(0, 64), :] = halo_d[...].astype(F32)
        vr, vi = ur, ui
        for t in range(3):
            r = ftmp[1, pl.ds(t, NJ, stride=8), :]
            e = jnp.exp(r)
            vr, vi = cmul(e * cr, -e * ci, vr, vi)
            s = scale_of(r)
            g_f[T + t, 0] = s * vr
            g_f[T + t, 1] = s * vi
            a, b = pair(ftmp.at[0], t)
            vr, vi = vr - a, vi - b

    @pl.when(last)
    def _():
        for t in range(3):
            g_f[T + t, 0] = zero
            g_f[T + t, 1] = zero

    init = [None] * CHUNKS
    for c in reversed(range(CHUNKS)):
        init[c] = (ur, ui)
        ar, ai, sr, si = chunk_maps[c]
        ur, ui = cmul(ar, ai, ur, ui)
        ur, ui = ur + sr, ui + si

    def pass2(n, st):
        st = list(st)
        for u in reversed(range(8)):
            for c in range(CHUNKS):
                t8 = c * (L // 8) + L // 8 - 1 - n
                t = t8 * 8 + u
                ur, ui = st[2 * c : 2 * c + 2]
                a, b = pair(cot_f, t)
                a, b = a + ur, b + ui
                s = sc_f[at(t8, u), :]
                g_f[t, 0] = s * a
                g_f[t, 1] = s * b
                e = e_f[at(t8, u), :]
                st[2 * c : 2 * c + 2] = cmul(e * cr, e * ci, a, b)
        return tuple(st)

    lax.fori_loop(0, L // 8, pass2, tuple(v for u in init for v in u))

    def taps(i, acc):
        acc = list(acc)
        for p in range(2):
            g = [g_f[i * 8 + k, p] for k in range(3)]
            for u in range(8):
                g.append(g_f[i * 8 + u + 3, p])
                x = x_f[pl.ds(2 * NJ * (i * 8 + u) + p, NJ, stride=2), :]
                for k in range(4):
                    acc[2 * k + p] = acc[2 * k + p] + g[u + k] * x
        return tuple(acc)

    acc = lax.fori_loop(0, T // 8, taps, (zero,) * 8)
    for k in range(4):
        for p in range(2):
            for jt in range(NJ):
                tbuf[2 * NJ * k + 2 * jt + p] = acc[2 * k + p][jt : jt + 1, :]
    trcv[me] = tbuf[me]

    def t1(dst_dev):
        return pltpu.make_async_remote_copy(
            src_ref=tbuf.at[dst_dev], dst_ref=trcv.at[me], send_sem=t1_s, recv_sem=t1_r,
            device_id=(dst_dev, ch), device_id_type=MESH)

    def t2(dst_dev):
        return pltpu.make_async_remote_copy(
            src_ref=trow, dst_ref=tap_ref.at[me], send_sem=t2_s, recv_sem=t2_r,
            device_id=(dst_dev, ch), device_id_type=MESH)

    def others(fn):
        def body(s, _):
            j = me + s
            fn(jnp.where(j >= n_seq, j - n_seq, j))
            return 0

        lax.fori_loop(1, n_seq, body, 0)

    others(lambda j: t1(j).start())

    cw = [[cw_ref[pl.ds(2 * NJ * k + p, NJ, stride=2), :] for p in range(2)] for k in range(4)]

    def conv(i, _):
        for p in range(2):
            g = [g_f[i * 16 + k, p] for k in range(3)]
            for u in range(16):
                g.append(g_f[i * 16 + u + 3, p])
                f = cw[0][p] * g[u] + cw[1][p] * g[u + 1] + cw[2][p] * g[u + 2] + cw[3][p] * g[u + 3]
                ftmp[p, pl.ds((u // 8) * 8 * NJ + u % 8, NJ, stride=8), :] = f
            for jt in range(NJ):
                v = jnp.concatenate([ftmp[p, pl.ds(jt * 8, 8), :], ftmp[p, pl.ds(8 * NJ + jt * 8, 8), :]], 0)
                feat[p * NJ + jt, pl.ds(pl.multiple_of(i * 16, 16), 16), :] = v.astype(BF16)
        return 0

    lax.fori_loop(0, T // 16, conv, 0)

    own = C // n_seq
    per = 128 // own

    def a2a_src(dst_dev):
        return featT.at[:, pl.ds(pl.multiple_of(dst_dev * own, own), own), :]

    cm_mine = cm_h.at[:, :, pl.ds(pl.multiple_of(me * T, T), T)]

    def a2a_copy(dst_dev):
        return pltpu.make_async_remote_copy(
            src_ref=a2a_src(dst_dev), dst_ref=cm_mine, send_sem=a2a_s, recv_sem=a2a_r,
            device_id=(dst_dev, ch), device_id_type=MESH)

    local = pltpu.make_async_copy(a2a_src(me), cm_mine, loc_s)

    def turn(s, _):
        jt = me // per + s
        jt = jnp.where(jt >= NJ, jt - NJ, jt)
        for p in range(2):
            featT[p, pl.ds(pl.multiple_of(jt * 128, 128), 128), :] = feat[p * NJ + jt].T
        for q in range(per):
            j = jt * per + q

            @pl.when(j != me)
            def _():
                a2a_copy(j).start()

        return 0

    lax.fori_loop(0, NJ, turn, 0)
    local.start()

    for i in range(W3, WCH):
        unpack_w(i)

    nt = D // NT
    half = T // 2

    def par_copy(n):
        cols = pl.ds(pl.multiple_of(n * nt, nt), nt)
        return pltpu.make_async_remote_copy(
            src_ref=part.at[pl.ds(pl.multiple_of(other * half, half), half), cols], dst_ref=part_r.at[:, cols],
            send_sem=par_s.at[n], recv_sem=par_r.at[n], device_id=(me, other), device_id_type=MESH)

    def tile(n, _):
        rows = pl.ds(pl.multiple_of(n * nt, nt), nt)
        lhs = jnp.concatenate([feat[i] for i in range(2 * NJ)], 1)
        rhs = jnp.concatenate([wk[i, rows, :] for i in range(2 * NJ)], 1)
        y = lax.dot_general(lhs, rhs, (((1,), (1,)), ((), ())), preferred_element_type=F32)
        part[:, rows] = y.astype(BF16)
        par_copy(n).start()
        return 0

    lax.fori_loop(0, NT // 2, tile, 0)

    def all_but_one(ref, sem):
        part_of = ref.at[pl.ds(0, n_seq - 1)]
        return pltpu.make_async_copy(part_of, part_of, sem)

    all_but_one(trcv, t1_r).wait()
    row = jnp.sum(trcv[...], axis=0)
    trow[...] = row
    tap_ref[me] = row
    others(lambda j: t2(j).start())

    lax.fori_loop(NT // 2, NT, tile, 0)

    def out_copy(n):
        cols = pl.ds(pl.multiple_of(n * nt, nt), nt)
        return pltpu.make_async_copy(obuf.at[:, cols], out_h.at[:, cols], o_sem.at[n])

    def join(n, _):
        par_copy(n).wait_recv()
        cols = pl.ds(pl.multiple_of(n * nt, nt), nt)
        mine = part[pl.ds(pl.multiple_of(ch * half, half), half), cols]
        obuf[:, cols] = (mine.astype(F32) + part_r[:, cols].astype(F32)).astype(BF16)
        out_copy(n).start()
        return 0

    lax.fori_loop(0, NT, join, 0)

    for k in range(STAGES):
        for s in range(1, RING):
            map_copy(k, s).wait_send()

    @pl.when(me > 0)
    def _():
        for c in halo_copies(before):
            c.wait_send()

    def ends(n, _):
        par_copy(n).wait_send()
        out_copy(n).wait()
        return 0

    lax.fori_loop(0, NT, ends, 0)
    all_but_one(trcv, t1_s).wait()
    all_but_one(trcv, t2_s).wait()
    all_but_one(tap_ref, t2_r).wait()
    local.wait()
    sent = featT.at[:, pl.ds(0, C - own), :]
    pltpu.make_async_copy(sent, sent, a2a_s).wait()
    came = cm_h.at[:, :, pl.ds(0, T * (n_seq - 1))]
    pltpu.make_async_copy(came, came, a2a_r).wait()


def solution(mesh):
    n_seq = mesh.shape["seq"]

    def flat(a):
        lead = a.shape[0]
        return a.reshape(lead, 2, -1, 128).transpose(0, 2, 1, 3).reshape(-1, 128)

    def on_device(cotangent, conv_input, decay_rate, angle, conv_weight, in_weight):
        T, _, C = cotangent.shape
        D = in_weight.shape[0]
        NJ = C // 128
        dec = decay_rate.reshape(T // 8, 8, NJ, 128).transpose(0, 2, 1, 3).reshape(-1, 128)
        dma = pltpu.SemaphoreType.DMA
        ANY = pl.BlockSpec(memory_space=pl.ANY)
        V = pl.BlockSpec(memory_space=pltpu.VMEM)
        rows = 8 * NJ
        out, cm, tap = pl.pallas_call(
            functools.partial(kernel, n_seq, T, C, D),
            out_shape=(
                jax.ShapeDtypeStruct((T // 2, D), BF16),
                jax.ShapeDtypeStruct((2, C // n_seq, T * n_seq), BF16),
                jax.ShapeDtypeStruct((rows, 1, 128), F32),
            ),
            in_specs=[ANY, ANY, ANY, V, V, ANY],
            out_specs=(ANY, ANY, V),
            scratch_shapes=[
                pltpu.VMEM((T * 2 * NJ, 128), BF16),
                pltpu.VMEM((T * 2 * NJ, 128), BF16),
                pltpu.VMEM((T * NJ, 128), BF16),
                pltpu.VMEM((D * 2 * NJ, 128), BF16),
                pltpu.VMEM((64, 128), BF16),
                pltpu.VMEM((64, 128), BF16),
                pltpu.VMEM((T * 2 * NJ, 128), F32),
                pltpu.VMEM((T * 2 * NJ, 128), F32),
                pltpu.VMEM((T * NJ, 128), F32),
                pltpu.VMEM((T * NJ, 128), F32),
                pltpu.VMEM((T + 3, 2, NJ, 128), F32),
                pltpu.VMEM((UNR, 32 * NJ, 128), F32),
                pltpu.VMEM((2 * NJ, D, 128), BF16),
                pltpu.VMEM((2, 16 * NJ, 128), F32),
                pltpu.VMEM((2 * NJ, T, 128), BF16),
                pltpu.VMEM((2, C, T), BF16),
                pltpu.VMEM((STAGES, 3, NJ, 128), F32),
                pltpu.VMEM((STAGES, RING, 3, NJ, 128), F32),
                pltpu.VMEM((T, D), BF16),
                pltpu.VMEM((T // 2, D), BF16),
                pltpu.VMEM((T // 2, D), BF16),
                pltpu.VMEM((rows, 1, 128), F32),
                pltpu.VMEM((n_seq, 1, 128), F32),
                pltpu.VMEM((1, 128), F32),
                dma((3,)), dma((WCH,)), dma((2,)), dma((2,)),
                dma((STAGES, RING)), dma((STAGES, RING)), dma, dma, dma,
                dma((NT,)), dma((NT,)),
                dma, dma, dma, dma, dma((NT,)),
            ],
            compiler_params=pltpu.CompilerParams(
                collective_id=0, has_side_effects=True, vmem_limit_bytes=62 * 1024 * 1024),
        )(flat(cotangent), flat(conv_input), dec, angle.reshape(NJ, 128), flat(conv_weight), flat(in_weight))
        tap = tap.reshape(4, NJ, 2, 128).transpose(0, 2, 1, 3).reshape(4, 2, C)
        return out, cm, tap

    in_specs = (
        P("seq", None, "ch"),
        P("seq", None, "ch"),
        P("seq", "ch"),
        P("ch"),
        P(None, None, "ch"),
        P(None, None, "ch"),
    )
    out_specs = (P(("seq", "ch"), None), P(None, ("ch", "seq"), None), P(None, None, "ch"))
    return jax.shard_map(on_device, mesh=mesh, in_specs=in_specs, out_specs=out_specs, check_vma=False)
```

```python
import functools

import jax
import jax.numpy as jnp
from jax import lax
from jax.experimental import pallas as pl
from jax.experimental.pallas import tpu as pltpu
from jax.sharding import PartitionSpec as P

MESH = pl.DeviceIdType.MESH
F32 = jnp.float32
BF16 = jnp.bfloat16
CHUNKS = 8
WCH = 8
WSLOT = 4
W1, W2, W3 = 1, 3, 5
UNR = 2
FIN = 4
NT = 8
RING = 4
STAGES = 3


def cmul(ar, ai, br, bi):
    return ar * br - ai * bi, ar * bi + ai * br


def scale_of(r):
    y = 0.25 * r
    q = y * (1.0 - y * (1 / 2) * (1.0 - y * (1 / 3) * (1.0 - y * (1 / 4) * (1.0 - y * (1 / 5) * (1.0 - y * (1 / 6))))))
    q = q * (2.0 - q)
    q = q * (2.0 - q)
    q = q * (2.0 - q)
    return jnp.sqrt(q)


def kernel(
    n_seq, T, C, D,
    cot_h, x_h, dec_h, ang_h, cw_h, w_h,
    mine_h, part_r, cm_h, tap_ref,
    ang_ref, cw_ref, cot_b, x_b, dec_b, w_b, halo_c, halo_d,
    cot_f, x_f, e_f, sc_f, g_f, wtmp, wk, ftmp, feat, featT,
    mapv, maps, part, tbuf, trcv, trow,
    in_sem, w_sem, halo_s, halo_r, map_s, map_r, a2a_s, a2a_r, loc_s, par_s, par_r, t1_s, t1_r, t2_s, t2_r, o_sem,
):
    me = lax.axis_index("seq")
    ch = lax.axis_index("ch")
    other = 1 - ch
    NJ = C // 128
    L = T // CHUNKS
    strides = [RING**k for k in range(STAGES)]
    place = [lax.rem(me // st, RING) for st in strides]

    def ring(k, s):
        return me + (lax.rem(place[k] + s, RING) - place[k]) * strides[k]

    barrier = pltpu.get_barrier_semaphore()

    def greet(dev, core):
        pl.semaphore_signal(barrier, inc=1, device_id=(dev, core), device_id_type=MESH)

    for k in range(STAGES):
        for s in range(1, RING):
            greet(ring(k, s), ch)
    before, after = lax.rem(me + n_seq - 1, n_seq), lax.rem(me + 1, n_seq)
    greet(before, ch)
    greet(after, ch)
    greet(me, other)
    greetings = STAGES * (RING - 1) + 3

    c_dec = pltpu.make_async_copy(dec_h, dec_b, in_sem.at[0])
    c_cot = pltpu.make_async_copy(cot_h, cot_b, in_sem.at[1])
    c_x = pltpu.make_async_copy(x_h, x_b, in_sem.at[2])
    c_ang = pltpu.make_async_copy(ang_h, ang_ref, in_sem.at[3])
    c_cw = pltpu.make_async_copy(cw_h, cw_ref, in_sem.at[4])
    c_dec.start()
    c_ang.start()
    c_cot.start()
    c_x.start()
    c_cw.start()
    wrows = w_h.shape[0] // WCH

    def w_copy(i):
        return pltpu.make_async_copy(
            w_h.at[pl.ds(i * wrows, wrows)], w_b.at[i % WSLOT], w_sem.at[i % WSLOT])

    for i in range(WSLOT):
        w_copy(i).start()


    def rowwise(src, dst, fn):
        def body(i, _):
            r = pl.multiple_of(i * 64, 64)
            dst[pl.ds(r, 64), :] = fn(src[pl.ds(r, 64), :].astype(F32))
            return 0

        lax.fori_loop(0, src.shape[0] // 64, body, 0)

    def pair(ref, t):
        return ref[pl.ds(2 * NJ * t, NJ, stride=2), :], ref[pl.ds(2 * NJ * t + 1, NJ, stride=2), :]

    c_dec.wait()
    rowwise(dec_b, e_f, lambda r: jnp.exp(-r))
    c_ang.wait()
    ang = ang_ref[...]
    cr = jnp.cos(ang)
    ci = -jnp.sin(ang)
    c_cot.wait()
    rowwise(cot_b, cot_f, lambda v: v)

    zero = jnp.zeros((NJ, 128), F32)
    one = jnp.ones((NJ, 128), F32)

    def at(t8, u):
        return pl.ds(8 * NJ * t8 + u, NJ, stride=8)

    def pass1(n, st):
        st = list(st)
        for u in reversed(range(8)):
            for c in range(CHUNKS):
                t8 = c * (L // 8) + L // 8 - 1 - n
                ur, ui, p = st[3 * c : 3 * c + 3]
                e = e_f[at(t8, u), :]
                a, b = pair(cot_f, t8 * 8 + u)
                ur, ui = cmul(e * cr, e * ci, a + ur, b + ui)
                st[3 * c : 3 * c + 3] = ur, ui, p * e
        return tuple(st)

    st = lax.fori_loop(0, L // 8, pass1, (zero, zero, one) * CHUNKS)

    def power(ar, ai, n):
        while n > 1:
            ar, ai = ar * ar - ai * ai, 2.0 * ar * ai
            n //= 2
        return ar, ai

    lr, li = power(cr, ci, L)
    rot = power(lr, li, CHUNKS)
    chunk_maps = []
    for c in range(CHUNKS):
        ur, ui, p = st[3 * c : 3 * c + 3]
        chunk_maps.append((p * lr, p * li, ur, ui))
    br, bi = zero, zero
    total = one
    for c in reversed(range(CHUNKS)):
        ar, ai, sr, si = chunk_maps[c]
        br, bi = cmul(ar, ai, br, bi)
        br, bi = br + sr, bi + si
        total = total * st[3 * c + 2]

    pl.semaphore_wait(barrier, greetings)

    def halo_copies(dst_dev):
        return [
            pltpu.make_async_remote_copy(
                src_ref=s, dst_ref=d, send_sem=halo_s.at[i], recv_sem=halo_r.at[i],
                device_id=(dst_dev, ch), device_id_type=MESH)
            for i, (s, d) in enumerate(
                ((cot_b.at[pl.ds(0, 64)], halo_c), (dec_b.at[pl.ds(0, 64)], halo_d)))
        ]

    def map_copy(k, s):
        return pltpu.make_async_remote_copy(
            src_ref=mapv.at[k], dst_ref=maps.at[k, place[k]], send_sem=map_s.at[k, s], recv_sem=map_r.at[k, RING - s],
            device_id=(ring(k, s), ch), device_id_type=MESH)

    def send_map(k, p, br, bi):
        for i, v in enumerate((p, br, bi)):
            mapv[k, i] = v
            maps[k, place[k], i] = v
        for s in range(1, RING):
            map_copy(k, s).start()

    def stage(k, rot):
        for s in range(1, RING):
            map_copy(k, s).wait_recv()
        ar, ai, br, bi, p = one, zero, zero, zero, one
        mine = None
        for j in reversed(range(RING)):
            here = place[k] == j
            now = (ar, ai, br, bi)
            mine = now if mine is None else tuple(jnp.where(here, x, y) for x, y in zip(now, mine))
            q = maps[k, j, 0]
            vr, vi = q * rot[0], q * rot[1]
            br, bi = cmul(vr, vi, br, bi)
            br, bi = br + maps[k, j, 1], bi + maps[k, j, 2]
            if j > 0:
                ar, ai = cmul(vr, vi, ar, ai)
            p = p * q
        return mine, (p, br, bi)

    send_map(0, total, br, bi)

    @pl.when(me > 0)
    def _():
        for c in halo_copies(before):
            c.start()

    G = 2 * NJ

    def unpack_w(i):
        w_copy(i).wait()
        base = i * (wrows // G)
        src = w_b.at[i % WSLOT]

        def body(k, _):
            for v in range(UNR):
                g = k * UNR + v
                d0 = pl.multiple_of(base + g * 16, 16)
                for d in range(16):
                    x = src[pl.ds(pl.multiple_of((g * 16 + d) * G, G), G), :].astype(F32)
                    for h in range(2):
                        wtmp[v, h, pl.ds(d * 8, 8), :] = x[h * 8 : h * 8 + 8, :]
                for p in range(2):
                    for jt in range(NJ):
                        x = wtmp[v, jt // 4, pl.ds(2 * (jt % 4) + p, 16, stride=8), :]
                        wk[p * NJ + jt, pl.ds(d0, 16), :] = x.astype(BF16)
            return 0

        lax.fori_loop(0, wrows // (G * 16 * UNR), body, 0)
        if i + WSLOT < WCH:
            w_copy(i + WSLOT).start()

    rowwise(dec_b, sc_f, scale_of)
    c_x.wait()
    rowwise(x_b, x_f, lambda v: v)
    for i in range(0, W1):
        unpack_w(i)

    later0, whole0 = stage(0, rot)
    send_map(1, *whole0)
    for i in range(W1, W2):
        unpack_w(i)
    rot1 = power(*rot, RING)
    later1, whole1 = stage(1, rot1)
    send_map(2, *whole1)
    for i in range(W2, W3):
        unpack_w(i)
    later2, _ = stage(2, power(*rot1, RING))

    ur, ui = later2[2], later2[3]
    for ar, ai, br, bi in (later1, later0):
        ur, ui = cmul(ar, ai, ur, ui)
        ur, ui = ur + br, ui + bi

    last = me == n_seq - 1

    @pl.when(jnp.logical_not(last))
    def _():
        for c in halo_copies(before):
            c.wait_recv()
        ftmp[0, pl.ds(0, 64), :] = halo_c[...].astype(F32)
        ftmp[1, pl.ds(0, 64), :] = halo_d[...].astype(F32)
        vr, vi = ur, ui
        for t in range(3):
            r = ftmp[1, pl.ds(t, NJ, stride=8), :]
            e = jnp.exp(r)
            vr, vi = cmul(e * cr, -e * ci, vr, vi)
            s = scale_of(r)
            g_f[T + t, 0] = s * vr
            g_f[T + t, 1] = s * vi
            a, b = pair(ftmp.at[0], t)
            vr, vi = vr - a, vi - b

    @pl.when(last)
    def _():
        for t in range(3):
            g_f[T + t, 0] = zero
            g_f[T + t, 1] = zero

    init = [None] * CHUNKS
    for c in reversed(range(CHUNKS)):
        init[c] = (ur, ui)
        ar, ai, sr, si = chunk_maps[c]
        ur, ui = cmul(ar, ai, ur, ui)
        ur, ui = ur + sr, ui + si

    def pass2(n, st):
        st = list(st)
        for u in reversed(range(8)):
            for c in range(CHUNKS):
                t8 = c * (L // 8) + L // 8 - 1 - n
                t = t8 * 8 + u
                ur, ui = st[2 * c : 2 * c + 2]
                a, b = pair(cot_f, t)
                a, b = a + ur, b + ui
                s = sc_f[at(t8, u), :]
                g_f[t, 0] = s * a
                g_f[t, 1] = s * b
                e = e_f[at(t8, u), :]
                st[2 * c : 2 * c + 2] = cmul(e * cr, e * ci, a, b)
        return tuple(st)

    lax.fori_loop(0, L // 8, pass2, tuple(v for u in init for v in u))

    def taps(i, acc):
        acc = list(acc)
        for p in range(2):
            g = [g_f[i * 8 + k, p] for k in range(3)]
            for u in range(8):
                g.append(g_f[i * 8 + u + 3, p])
                x = x_f[pl.ds(2 * NJ * (i * 8 + u) + p, NJ, stride=2), :]
                for k in range(4):
                    acc[2 * k + p] = acc[2 * k + p] + g[u + k] * x
        return tuple(acc)

    acc = lax.fori_loop(0, T // 8, taps, (zero,) * 8)
    for k in range(4):
        for p in range(2):
            for jt in range(NJ):
                tbuf[2 * NJ * k + 2 * jt + p] = acc[2 * k + p][jt : jt + 1, :]
    trcv[me] = tbuf[me]

    def t1(dst_dev):
        return pltpu.make_async_remote_copy(
            src_ref=tbuf.at[dst_dev], dst_ref=trcv.at[me], send_sem=t1_s, recv_sem=t1_r,
            device_id=(dst_dev, ch), device_id_type=MESH)

    def t2(dst_dev):
        return pltpu.make_async_remote_copy(
            src_ref=trow, dst_ref=tap_ref.at[me], send_sem=t2_s, recv_sem=t2_r,
            device_id=(dst_dev, ch), device_id_type=MESH)

    def others(fn):
        def body(s, _):
            j = me + s
            fn(jnp.where(j >= n_seq, j - n_seq, j))
            return 0

        lax.fori_loop(1, n_seq, body, 0)

    others(lambda j: t1(j).start())

    c_cw.wait()
    cw = [[cw_ref[pl.ds(2 * NJ * k + p, NJ, stride=2), :] for p in range(2)] for k in range(4)]

    def conv(i, _):
        for p in range(2):
            g = [g_f[i * 16 + k, p] for k in range(3)]
            for u in range(16):
                g.append(g_f[i * 16 + u + 3, p])
                f = cw[0][p] * g[u] + cw[1][p] * g[u + 1] + cw[2][p] * g[u + 2] + cw[3][p] * g[u + 3]
                ftmp[p, pl.ds((u // 8) * 8 * NJ + u % 8, NJ, stride=8), :] = f
            for jt in range(NJ):
                v = jnp.concatenate([ftmp[p, pl.ds(jt * 8, 8), :], ftmp[p, pl.ds(8 * NJ + jt * 8, 8), :]], 0)
                feat[p * NJ + jt, pl.ds(pl.multiple_of(i * 16, 16), 16), :] = v.astype(BF16)
        return 0

    lax.fori_loop(0, T // 16, conv, 0)

    own = C // n_seq
    per = 128 // own

    def a2a_src(dst_dev):
        return featT.at[:, pl.ds(pl.multiple_of(dst_dev * own, own), own), :]

    cm_mine = cm_h.at[:, :, pl.ds(pl.multiple_of(me * T, T), T)]

    def a2a_copy(dst_dev):
        return pltpu.make_async_remote_copy(
            src_ref=a2a_src(dst_dev), dst_ref=cm_mine, send_sem=a2a_s, recv_sem=a2a_r,
            device_id=(dst_dev, ch), device_id_type=MESH)

    local = pltpu.make_async_copy(a2a_src(me), cm_mine, loc_s)

    def turn(s, _):
        jt = me // per + s
        jt = jnp.where(jt >= NJ, jt - NJ, jt)
        for p in range(2):
            featT[p, pl.ds(pl.multiple_of(jt * 128, 128), 128), :] = feat[p * NJ + jt].T
        for q in range(per):
            j = jt * per + q

            @pl.when(j != me)
            def _():
                a2a_copy(j).start()

        return 0

    lax.fori_loop(0, NJ, turn, 0)
    local.start()

    for i in range(W3, WCH):
        unpack_w(i)

    nt = D // NT
    half = T // 2

    def par_copy(n):
        cols = pl.ds(pl.multiple_of(n * nt, nt), nt)
        return pltpu.make_async_remote_copy(
            src_ref=part.at[pl.ds(pl.multiple_of(other * half, half), half), cols], dst_ref=part_r.at[:, cols],
            send_sem=par_s.at[n], recv_sem=par_r.at[n], device_id=(me, other), device_id_type=MESH)

    def tile(n, _):
        rows = pl.ds(pl.multiple_of(n * nt, nt), nt)
        lhs = jnp.concatenate([feat[i] for i in range(2 * NJ)], 1)
        rhs = jnp.concatenate([wk[i, rows, :] for i in range(2 * NJ)], 1)
        y = lax.dot_general(lhs, rhs, (((1,), (1,)), ((), ())), preferred_element_type=F32)
        part[:, rows] = y.astype(BF16)
        par_copy(n).start()
        return 0

    lax.fori_loop(0, NT // 2, tile, 0)

    def all_but_one(ref, sem):
        part_of = ref.at[pl.ds(0, n_seq - 1)]
        return pltpu.make_async_copy(part_of, part_of, sem)

    all_but_one(trcv, t1_r).wait()
    row = jnp.sum(trcv[...], axis=0)
    trow[...] = row
    tap_ref[me] = row
    others(lambda j: t2(j).start())

    lax.fori_loop(NT // 2, NT, tile, 0)

    mine = pltpu.make_async_copy(part.at[pl.ds(pl.multiple_of(ch * half, half), half), :], mine_h, o_sem)
    mine.start()

    for k in range(STAGES):
        for s in range(1, RING):
            map_copy(k, s).wait_send()

    @pl.when(me > 0)
    def _():
        for c in halo_copies(before):
            c.wait_send()

    def ends(n, _):
        par_copy(n).wait()
        return 0

    lax.fori_loop(0, NT, ends, 0)
    mine.wait()
    all_but_one(trcv, t1_s).wait()
    all_but_one(trcv, t2_s).wait()
    all_but_one(tap_ref, t2_r).wait()
    local.wait()
    sent = featT.at[:, pl.ds(0, C - own), :]
    pltpu.make_async_copy(sent, sent, a2a_s).wait()
    came = cm_h.at[:, :, pl.ds(0, T * (n_seq - 1))]
    pltpu.make_async_copy(came, came, a2a_r).wait()


def finish(mine, part, cm, tap, out_h, cm_h, tap_h, out, sem):
    rows = mine.shape[0] // FIN
    copies = [pltpu.make_async_copy(cm.at[p], cm_h.at[p], sem.at[FIN + p]) for p in range(2)]
    copies.append(pltpu.make_async_copy(tap, tap_h, sem.at[FIN + 2]))
    for c in copies:
        c.start()
    for i in range(FIN):
        r = pl.ds(i * rows, rows)
        out[r, :] = (mine[r, :].astype(F32) + part[r, :].astype(F32)).astype(BF16)
        copies.append(pltpu.make_async_copy(out.at[r], out_h.at[r], sem.at[i]))
        copies[-1].start()
    for c in copies:
        c.wait()


def solution(mesh):
    n_seq = mesh.shape["seq"]

    def flat(a):
        lead = a.shape[0]
        return a.reshape(lead, 2, -1, 128).transpose(0, 2, 1, 3).reshape(-1, 128)

    def on_device(cotangent, conv_input, decay_rate, angle, conv_weight, in_weight):
        T, _, C = cotangent.shape
        D = in_weight.shape[0]
        NJ = C // 128
        dec = decay_rate.reshape(T // 8, 8, NJ, 128).transpose(0, 2, 1, 3).reshape(-1, 128)
        dma = pltpu.SemaphoreType.DMA
        ANY = pl.BlockSpec(memory_space=pl.ANY)
        V = pl.BlockSpec(memory_space=pltpu.VMEM)
        rows = 8 * NJ
        HBM = pl.BlockSpec(memory_space=pltpu.HBM)
        mine, part, cm, tap = pl.pallas_call(
            functools.partial(kernel, n_seq, T, C, D),
            out_shape=(
                jax.ShapeDtypeStruct((T // 2, D), BF16),
                jax.ShapeDtypeStruct((T // 2, D), BF16),
                jax.ShapeDtypeStruct((2, C // n_seq, T * n_seq), BF16),
                jax.ShapeDtypeStruct((rows, 1, 128), F32),
            ),
            in_specs=[HBM] * 6,
            out_specs=(ANY, ANY, ANY, V),
            scratch_shapes=[
                pltpu.VMEM((NJ, 128), F32),
                pltpu.VMEM((8 * NJ, 128), F32),
                pltpu.VMEM((T * 2 * NJ, 128), BF16),
                pltpu.VMEM((T * 2 * NJ, 128), BF16),
                pltpu.VMEM((T * NJ, 128), BF16),
                pltpu.VMEM((WSLOT, D * 2 * NJ // WCH, 128), BF16),
                pltpu.VMEM((64, 128), BF16),
                pltpu.VMEM((64, 128), BF16),
                pltpu.VMEM((T * 2 * NJ, 128), F32),
                pltpu.VMEM((T * 2 * NJ, 128), F32),
                pltpu.VMEM((T * NJ, 128), F32),
                pltpu.VMEM((T * NJ, 128), F32),
                pltpu.VMEM((T + 3, 2, NJ, 128), F32),
                pltpu.VMEM((UNR, 2, 128, 128), F32),
                pltpu.VMEM((2 * NJ, D, 128), BF16),
                pltpu.VMEM((2, 16 * NJ, 128), F32),
                pltpu.VMEM((2 * NJ, T, 128), BF16),
                pltpu.VMEM((2, C, T), BF16),
                pltpu.VMEM((STAGES, 3, NJ, 128), F32),
                pltpu.VMEM((STAGES, RING, 3, NJ, 128), F32),
                pltpu.VMEM((T, D), BF16),
                pltpu.VMEM((rows, 1, 128), F32),
                pltpu.VMEM((n_seq, 1, 128), F32),
                pltpu.VMEM((1, 128), F32),
                dma((5,)), dma((WSLOT,)), dma((2,)), dma((2,)),
                dma((STAGES, RING)), dma((STAGES, RING)), dma, dma, dma,
                dma((NT,)), dma((NT,)),
                dma, dma, dma, dma, dma,
            ],
            compiler_params=pltpu.CompilerParams(
                collective_id=0, has_side_effects=True, vmem_limit_bytes=46 * 1024 * 1024),
        )(*[
                pltpu.with_memory_space_constraint(v, pltpu.HBM)
                for v in (flat(cotangent), flat(conv_input), dec, angle.reshape(NJ, 128), flat(conv_weight), flat(in_weight))
            ])
        out, cm, tap = pl.pallas_call(
            finish,
            out_shape=(
                jax.ShapeDtypeStruct((T // 2, D), BF16),
                jax.ShapeDtypeStruct(cm.shape, BF16),
                jax.ShapeDtypeStruct(tap.shape, F32),
            ),
            in_specs=[V] * 4,
            out_specs=(HBM, HBM, HBM),
            scratch_shapes=[pltpu.VMEM((T // 2, D), BF16), dma((FIN + 3,))],
            compiler_params=pltpu.CompilerParams(vmem_limit_bytes=16 * 1024 * 1024),
        )(mine, part, cm, tap)
        tap = tap.reshape(4, NJ, 2, 128).transpose(0, 2, 1, 3).reshape(4, 2, C)
        return out, cm, tap

    in_specs = (
        P("seq", None, "ch"),
        P("seq", None, "ch"),
        P("seq", "ch"),
        P("ch"),
        P(None, None, "ch"),
        P(None, None, "ch"),
    )
    out_specs = (P(("seq", "ch"), None), P(None, ("ch", "seq"), None), P(None, None, "ch"))
    return jax.shard_map(on_device, mesh=mesh, in_specs=in_specs, out_specs=out_specs, check_vma=False)
```

```python
import functools

import jax
import jax.numpy as jnp
from jax import lax
from jax.experimental import pallas as pl
from jax.experimental.pallas import tpu as pltpu
from jax.sharding import PartitionSpec as P

MESH = pl.DeviceIdType.MESH
F32 = jnp.float32
BF16 = jnp.bfloat16
CHUNKS = 8
WCH = 2
WSLOT = 1
W1, W2, W3, W4 = 0, 1, 1, 2
H1, H2 = 2, 2
S2 = 8
PAD = 64
FIN = 4
NT = 8
RING = 4
STAGES = 3


def cmul(ar, ai, br, bi):
    return ar * br - ai * bi, ar * bi + ai * br


def scale_of(r):
    y = 0.25 * r
    q = y * (1.0 - y * (1 / 2) * (1.0 - y * (1 / 3) * (1.0 - y * (1 / 4) * (1.0 - y * (1 / 5) * (1.0 - y * (1 / 6))))))
    q = q * (2.0 - q)
    q = q * (2.0 - q)
    q = q * (2.0 - q)
    return jnp.sqrt(q)


def kernel(
    n_seq, T, C, D,
    cot_h, x_h, dec_h, ang_h, cw_h, w_h,
    mine_h, part_r, cm_h, tap_ref,
    ang_ref, cw_ref, cot_b, x_b, dec_b, w_b, halo,
    cot_f, x_f, e_f, sc_f, g_f, seed, sums, perm, wk, ftmp, feat, featT,
    mapv, maps, part, tbuf, trcv, trow,
    in_sem, w_sem, halo_s, halo_r, map_s, map_r, a2a_s, a2a_r, loc_s, par_s, par_r, t1_s, t1_r, t2_s, t2_r, o_sem,
):
    me = lax.axis_index("seq")
    ch = lax.axis_index("ch")
    other = 1 - ch
    NJ = C // 128
    L = T // CHUNKS
    strides = [RING**k for k in range(STAGES)]
    place = [lax.rem(me // st, RING) for st in strides]

    def ring(k, s):
        return me + (lax.rem(place[k] + s, RING) - place[k]) * strides[k]

    barrier = pltpu.get_barrier_semaphore()

    def greet(dev, core):
        pl.semaphore_signal(barrier, inc=1, device_id=(dev, core), device_id_type=MESH)

    for k in range(STAGES):
        for s in range(1, RING):
            greet(ring(k, s), ch)
    greet(me, other)
    greetings = STAGES * (RING - 1) + 1

    c_dec = pltpu.make_async_copy(dec_h, dec_b, in_sem.at[0])
    c_cot = pltpu.make_async_copy(cot_h, cot_b, in_sem.at[1])
    c_x = pltpu.make_async_copy(x_h, x_b, in_sem.at[2])
    c_ang = pltpu.make_async_copy(ang_h, ang_ref, in_sem.at[3])
    c_cw = pltpu.make_async_copy(cw_h, cw_ref, in_sem.at[4])
    c_dec.start()
    c_ang.start()
    c_cot.start()
    c_x.start()
    c_cw.start()
    wrows = w_h.shape[0] // WCH

    def w_copy(i):
        return pltpu.make_async_copy(
            w_h.at[pl.ds(i * wrows, wrows)], w_b.at[i % WSLOT], w_sem.at[i % WSLOT])

    for i in range(WSLOT):
        w_copy(i).start()


    def rowwise(src, dst, fn):
        def body(i, _):
            r = pl.multiple_of(i * 64, 64)
            dst[pl.ds(r, 64), :] = fn(src[pl.ds(r, 64), :].astype(F32))
            return 0

        lax.fori_loop(0, src.shape[0] // 64, body, 0)

    def pair(ref, t):
        return ref[pl.ds(2 * NJ * t, NJ, stride=2), :], ref[pl.ds(2 * NJ * t + 1, NJ, stride=2), :]

    c_dec.wait()
    rowwise(dec_b, e_f, lambda r: jnp.exp(-r))
    c_ang.wait()
    ang = ang_ref[...]
    cr = jnp.cos(ang)
    ci = -jnp.sin(ang)
    c_cot.wait()
    rowwise(cot_b, cot_f, lambda v: v)

    zero = jnp.zeros((NJ, 128), F32)
    one = jnp.ones((NJ, 128), F32)

    def at(t8, u):
        return pl.ds(8 * NJ * t8 + u, NJ, stride=8)

    def pass1(n, st):
        st = list(st)
        for u in reversed(range(8)):
            for c in range(CHUNKS):
                t8 = c * (L // 8) + L // 8 - 1 - n
                ur, ui, p = st[3 * c : 3 * c + 3]
                e = e_f[at(t8, u), :]
                a, b = pair(cot_f, t8 * 8 + u)
                ur, ui = cmul(e * cr, e * ci, a + ur, b + ui)
                st[3 * c : 3 * c + 3] = ur, ui, p * e
        return tuple(st)

    st = lax.fori_loop(0, L // 8, pass1, (zero, zero, one) * CHUNKS)

    def power(ar, ai, n):
        while n > 1:
            ar, ai = ar * ar - ai * ai, 2.0 * ar * ai
            n //= 2
        return ar, ai

    lr, li = power(cr, ci, L)
    rot = power(lr, li, CHUNKS)
    chunk_maps = []
    for c in range(CHUNKS):
        ur, ui, p = st[3 * c : 3 * c + 3]
        chunk_maps.append((p * lr, p * li, ur, ui))
    br, bi = zero, zero
    total = one
    for c in reversed(range(CHUNKS)):
        ar, ai, sr, si = chunk_maps[c]
        br, bi = cmul(ar, ai, br, bi)
        br, bi = br + sr, bi + si
        total = total * st[3 * c + 2]

    raw = dec_b[pl.ds(0, 8 * NJ), :].astype(F32)
    ftmp[0, pl.ds(0, 8 * NJ), :] = raw
    halo[0, pl.ds(0, 32), :] = cot_b[pl.ds(0, 32), :]
    firsts = [ftmp[0, pl.ds(t, NJ, stride=8), :] for t in range(3)]
    halo[0, pl.ds(32, 32), :] = jnp.concatenate(firsts + firsts[2:], 0).astype(BF16)
    pl.semaphore_wait(barrier, greetings)

    def halo_copy(k):
        return pltpu.make_async_remote_copy(
            src_ref=halo.at[k], dst_ref=halo.at[k + 1], send_sem=halo_s.at[k], recv_sem=halo_r.at[k],
            device_id=(ring(k, RING - 1), ch), device_id_type=MESH)

    edge = [None]
    for k in range(1, STAGES):
        top = place[k - 1] == RING - 1
        edge.append(top if k == 1 else jnp.logical_and(edge[-1], top))

    def passing(k, act):
        if k == 0:
            act(halo_copy(0))
        else:

            @pl.when(edge[k])
            def _():
                act(halo_copy(k))

    def map_copy(k, s):
        return pltpu.make_async_remote_copy(
            src_ref=mapv.at[k], dst_ref=maps.at[k, place[k]], send_sem=map_s.at[k, s], recv_sem=map_r.at[k, RING - s],
            device_id=(ring(k, s), ch), device_id_type=MESH)

    def send_map(k, p, br, bi):
        for i, v in enumerate((p, br, bi)):
            mapv[k, i] = v
            maps[k, place[k], i] = v
        for s in range(1, RING):
            map_copy(k, s).start()
        if k > 0:
            passing(k - 1, lambda c: c.wait_recv())
        passing(k, lambda c: c.start())

    def stage(k, rot):
        for s in range(1, RING):
            map_copy(k, s).wait_recv()
        ar, ai, br, bi, p = one, zero, zero, zero, one
        mine = None
        for j in reversed(range(RING)):
            here = place[k] == j
            now = (ar, ai, br, bi)
            mine = now if mine is None else tuple(jnp.where(here, x, y) for x, y in zip(now, mine))
            q = maps[k, j, 0]
            vr, vi = q * rot[0], q * rot[1]
            br, bi = cmul(vr, vi, br, bi)
            br, bi = br + maps[k, j, 1], bi + maps[k, j, 2]
            if j > 0:
                ar, ai = cmul(vr, vi, ar, ai)
            p = p * q
        return mine, (p, br, bi)

    send_map(0, total, br, bi)

    G = 32 * NJ
    r, c = (lax.broadcasted_iota(jnp.int32, (G, G), d) for d in range(2))
    plane, row = r // 16, r % 16
    perm[...] = (c == row * 2 * NJ + (plane % NJ) * 2 + plane // NJ).astype(F32).astype(BF16)

    def unpack_w(i):
        w_copy(i).wait()
        src = w_b.at[i % WSLOT]
        n = wrows // G
        x = jnp.concatenate([src[pl.ds(v * G, G), :] for v in range(n)], 1)
        y = jnp.dot(perm[...], x, preferred_element_type=F32).astype(BF16)
        for v in range(n):
            for q in range(2 * NJ):
                wk[q, pl.ds((i * n + v) * 16, 16), :] = y[q * 16 : q * 16 + 16, v * 128 : v * 128 + 128]
        if i + WSLOT < WCH:
            w_copy(i + WSLOT).start()

    rowwise(dec_b, sc_f, scale_of)
    c_x.wait()
    x_f[pl.ds(0, PAD), :] = jnp.zeros((PAD, 128), F32)

    def spread(i, _):
        r = pl.multiple_of(i * 64, 64)
        x_f[pl.ds(PAD + r, 64), :] = x_b[pl.ds(r, 64), :].astype(F32)
        return 0

    lax.fori_loop(0, x_b.shape[0] // 64, spread, 0)

    b, q = (zero, zero), (one, zero)
    for c in reversed(range(CHUNKS)):
        for i, v in enumerate(b + q):
            seed[c, i] = v
        ar, ai, sr, si = chunk_maps[c]
        b = cmul(ar, ai, *b)
        b = b[0] + sr, b[1] + si
        q = cmul(ar, ai, *q)
    for i in range(24):
        sums[i] = zero

    def split(lo, hi):
        def two(h, _):
            def body(n, st):
                st = list(st)
                xs = {}
                for u in reversed(range(8)):
                    for v in range(2):
                        t8 = (2 * h + v) * (L // 8) + L // 8 - 1 - n
                        t = t8 * 8 + u
                        br, bi, qr, qi = st[4 * v : 4 * v + 4]
                        a, b = pair(cot_f, t)
                        br, bi = a + br, b + bi
                        s = sc_f[at(t8, u), :]
                        vals = (s * br, s * bi, s * qr, s * qi)
                        for i, w in enumerate(vals):
                            g_f[t, i] = w
                        for k in range(4):
                            if (v, u - k) not in xs:
                                xs[v, u - k] = pair(x_f.at[pl.ds(pl.multiple_of(16 * t8 * NJ, 8), PAD + 16 * NJ)], u - k + PAD // (2 * NJ))
                            xr, xi = xs[v, u - k]
                            for i, w in enumerate((vals[0] * xr, vals[1] * xi, vals[2] * xr, vals[3] * xr, vals[2] * xi, vals[3] * xi)):
                                st[8 + 6 * k + i] = st[8 + 6 * k + i] + w
                        e = e_f[at(t8, u), :]
                        mr, mi = e * cr, e * ci
                        st[4 * v : 4 * v + 4] = (*cmul(mr, mi, br, bi), *cmul(mr, mi, qr, qi))
                return tuple(st)

            st = [seed[2 * h + v, i] for v in range(2) for i in range(4)]
            st = lax.fori_loop(0, L // 8, body, tuple(st + [sums[i] for i in range(24)]))
            for i in range(24):
                sums[i] = st[8 + i]
            return 0

        lax.fori_loop(lo, hi, two, 0)

    split(0, H1)
    for i in range(0, W1):
        unpack_w(i)

    later0, whole0 = stage(0, rot)
    send_map(1, *whole0)
    split(H1, H2)
    for i in range(W1, W2):
        unpack_w(i)
    rot1 = power(*rot, RING)
    later1, whole1 = stage(1, rot1)
    send_map(2, *whole1)
    split(H2, CHUNKS // 2)
    for i in range(W2, W3):
        unpack_w(i)
    later2, _ = stage(2, power(*rot1, RING))

    passing(STAGES - 1, lambda c: c.wait_recv())
    ur, ui = later2[2], later2[3]
    for ar, ai, br, bi in (later1, later0):
        ur, ui = cmul(ar, ai, ur, ui)
        ur, ui = ur + br, ui + bi

    last = me == n_seq - 1

    @pl.when(jnp.logical_not(last))
    def _():
        which = 1 + jnp.where(edge[1], 1, 0) + jnp.where(edge[2], 1, 0)
        rows = halo[which].astype(F32)
        ftmp[0, pl.ds(0, 64), :] = rows
        vr, vi = ur, ui
        for t in range(3):
            r = rows[32 + t * NJ : 32 + (t + 1) * NJ, :]
            e = jnp.exp(r)
            vr, vi = cmul(e * cr, -e * ci, vr, vi)
            s = scale_of(r)
            g_f[T + t, 0] = s * vr
            g_f[T + t, 1] = s * vi
            g_f[T + t, 2] = zero
            g_f[T + t, 3] = zero
            if t < 2:
                a, b = pair(ftmp.at[0], t)
                vr, vi = vr - a, vi - b

    @pl.when(last)
    def _():
        for t in range(3):
            for i in range(4):
                g_f[T + t, i] = zero

    for k in range(4):
        a = [sums[6 * k + i] for i in range(6)]
        acc = [a[0] + a[2] * ur - a[3] * ui, a[1] + a[4] * ui + a[5] * ur]
        for t in range(k):
            x = pair(x_f, T + t - k + PAD // (2 * NJ))
            for p in range(2):
                acc[p] = acc[p] + g_f[T + t, p] * x[p]
        for p in range(2):
            for jt in range(NJ):
                tbuf[2 * NJ * k + 2 * jt + p] = acc[p][jt : jt + 1, :]
    trcv[me] = tbuf[me]

    def t1(dst_dev):
        return pltpu.make_async_remote_copy(
            src_ref=tbuf.at[dst_dev], dst_ref=trcv.at[me], send_sem=t1_s, recv_sem=t1_r,
            device_id=(dst_dev, ch), device_id_type=MESH)

    def t2(dst_dev):
        return pltpu.make_async_remote_copy(
            src_ref=trow, dst_ref=tap_ref.at[me], send_sem=t2_s, recv_sem=t2_r,
            device_id=(dst_dev, ch), device_id_type=MESH)

    def others(fn):
        def body(s, _):
            j = me + s
            fn(jnp.where(j >= n_seq, j - n_seq, j))
            return 0

        lax.fori_loop(1, n_seq, body, 0)

    others(lambda j: t1(j).start())

    c_cw.wait()
    cw = [[cw_ref[pl.ds(2 * NJ * k + p, NJ, stride=2), :] for p in range(2)] for k in range(4)]

    def conv(i, _):
        def full(t):
            hr, hi = cmul(g_f[t, 2], g_f[t, 3], ur, ui)
            return g_f[t, 0] + hr, g_f[t, 1] + hi

        both = [full(i * 16 + k) for k in range(19)]
        for p in range(2):
            g = [v[p] for v in both]
            for u in range(16):
                f = cw[0][p] * g[u] + cw[1][p] * g[u + 1] + cw[2][p] * g[u + 2] + cw[3][p] * g[u + 3]
                ftmp[p, pl.ds((u // 8) * 8 * NJ + u % 8, NJ, stride=8), :] = f
            for jt in range(NJ):
                v = jnp.concatenate([ftmp[p, pl.ds(jt * 8, 8), :], ftmp[p, pl.ds(8 * NJ + jt * 8, 8), :]], 0)
                feat[p * NJ + jt, pl.ds(pl.multiple_of(i * 16, 16), 16), :] = v.astype(BF16)
        return 0

    lax.fori_loop(0, T // 16, conv, 0)

    own = C // n_seq
    per = 128 // own

    def a2a_src(dst_dev):
        return featT.at[:, pl.ds(pl.multiple_of(dst_dev * own, own), own), :]

    cm_mine = cm_h.at[:, :, pl.ds(pl.multiple_of(me * T, T), T)]

    def a2a_copy(dst_dev):
        return pltpu.make_async_remote_copy(
            src_ref=a2a_src(dst_dev), dst_ref=cm_mine, send_sem=a2a_s, recv_sem=a2a_r,
            device_id=(dst_dev, ch), device_id_type=MESH)

    local = pltpu.make_async_copy(a2a_src(me), cm_mine, loc_s)

    def turn(s, _):
        jt = me // per + s
        jt = jnp.where(jt >= NJ, jt - NJ, jt)
        for p in range(2):
            featT[p, pl.ds(pl.multiple_of(jt * 128, 128), 128), :] = feat[p * NJ + jt].T
        for q in range(per):
            j = jt * per + q

            @pl.when(j != me)
            def _():
                a2a_copy(j).start()

        return 0

    lax.fori_loop(0, S2, turn, 0)

    for i in range(W3, W4):
        unpack_w(i)

    def all_but_one(ref, sem):
        part_of = ref.at[pl.ds(0, n_seq - 1)]
        return pltpu.make_async_copy(part_of, part_of, sem)

    all_but_one(trcv, t1_r).wait()
    row = jnp.sum(trcv[...], axis=0)
    trow[...] = row
    tap_ref[me] = row
    others(lambda j: t2(j).start())

    for i in range(W4, WCH):
        unpack_w(i)

    lax.fori_loop(S2, NJ, turn, 0)
    local.start()

    nt = D // NT
    half = T // 2

    def par_copy(n):
        cols = pl.ds(pl.multiple_of(n * nt, nt), nt)
        return pltpu.make_async_remote_copy(
            src_ref=part.at[pl.ds(pl.multiple_of(other * half, half), half), cols], dst_ref=part_r.at[:, cols],
            send_sem=par_s.at[n], recv_sem=par_r.at[n], device_id=(me, other), device_id_type=MESH)

    def tile(n, _):
        rows = pl.ds(pl.multiple_of(n * nt, nt), nt)
        lhs = jnp.concatenate([feat[i] for i in range(2 * NJ)], 1)
        rhs = jnp.concatenate([wk[i, rows, :] for i in range(2 * NJ)], 1)
        y = lax.dot_general(lhs, rhs, (((1,), (1,)), ((), ())), preferred_element_type=F32)
        part[:, rows] = y.astype(BF16)
        par_copy(n).start()
        return 0

    lax.fori_loop(0, NT, tile, 0)


    mine = pltpu.make_async_copy(part.at[pl.ds(pl.multiple_of(ch * half, half), half), :], mine_h, o_sem)
    mine.start()

    for k in range(STAGES):
        for s in range(1, RING):
            map_copy(k, s).wait_send()

    for k in range(STAGES):
        passing(k, lambda c: c.wait_send())

    def ends(n, _):
        par_copy(n).wait()
        return 0

    lax.fori_loop(0, NT, ends, 0)
    mine.wait()
    all_but_one(trcv, t1_s).wait()
    all_but_one(trcv, t2_s).wait()
    all_but_one(tap_ref, t2_r).wait()
    local.wait()
    sent = featT.at[:, pl.ds(0, C - own), :]
    pltpu.make_async_copy(sent, sent, a2a_s).wait()
    came = cm_h.at[:, :, pl.ds(0, T * (n_seq - 1))]
    pltpu.make_async_copy(came, came, a2a_r).wait()


def finish(mine, part, cm, tap, out_h, cm_h, tap_h, out, sem):
    rows = mine.shape[0] // FIN
    copies = [pltpu.make_async_copy(cm.at[p], cm_h.at[p], sem.at[FIN + p]) for p in range(2)]
    copies.append(pltpu.make_async_copy(tap, tap_h, sem.at[FIN + 2]))
    for c in copies:
        c.start()
    for i in range(FIN):
        r = pl.ds(i * rows, rows)
        out[r, :] = (mine[r, :].astype(F32) + part[r, :].astype(F32)).astype(BF16)
        copies.append(pltpu.make_async_copy(out.at[r], out_h.at[r], sem.at[i]))
        copies[-1].start()
    for c in copies:
        c.wait()


def solution(mesh):
    n_seq = mesh.shape["seq"]

    def flat(a):
        lead = a.shape[0]
        return a.reshape(lead, 2, -1, 128).transpose(0, 2, 1, 3).reshape(-1, 128)

    def on_device(cotangent, conv_input, decay_rate, angle, conv_weight, in_weight):
        T, _, C = cotangent.shape
        D = in_weight.shape[0]
        NJ = C // 128
        dec = decay_rate.reshape(T // 8, 8, NJ, 128).transpose(0, 2, 1, 3).reshape(-1, 128)
        dma = pltpu.SemaphoreType.DMA
        ANY = pl.BlockSpec(memory_space=pl.ANY)
        V = pl.BlockSpec(memory_space=pltpu.VMEM)
        rows = 8 * NJ
        HBM = pl.BlockSpec(memory_space=pltpu.HBM)
        mine, part, cm, tap = pl.pallas_call(
            functools.partial(kernel, n_seq, T, C, D),
            out_shape=(
                jax.ShapeDtypeStruct((T // 2, D), BF16),
                jax.ShapeDtypeStruct((T // 2, D), BF16),
                jax.ShapeDtypeStruct((2, C // n_seq, T * n_seq), BF16),
                jax.ShapeDtypeStruct((rows, 1, 128), F32),
            ),
            in_specs=[HBM] * 6,
            out_specs=(ANY, ANY, ANY, V),
            scratch_shapes=[
                pltpu.VMEM((NJ, 128), F32),
                pltpu.VMEM((8 * NJ, 128), F32),
                pltpu.VMEM((T * 2 * NJ, 128), BF16),
                pltpu.VMEM((T * 2 * NJ, 128), BF16),
                pltpu.VMEM((T * NJ, 128), BF16),
                pltpu.VMEM((WSLOT, D * 2 * NJ // WCH, 128), BF16),
                pltpu.VMEM((STAGES + 1, 64, 128), BF16),
                pltpu.VMEM((T * 2 * NJ, 128), F32),
                pltpu.VMEM((T * 2 * NJ + PAD, 128), F32),
                pltpu.VMEM((T * NJ, 128), F32),
                pltpu.VMEM((T * NJ, 128), F32),
                pltpu.VMEM((T + 3, 4, NJ, 128), F32),
                pltpu.VMEM((CHUNKS, 4, NJ, 128), F32),
                pltpu.VMEM((24, NJ, 128), F32),
                pltpu.VMEM((32 * NJ, 32 * NJ), BF16),
                pltpu.VMEM((2 * NJ, D, 128), BF16),
                pltpu.VMEM((2, 16 * NJ, 128), F32),
                pltpu.VMEM((2 * NJ, T, 128), BF16),
                pltpu.VMEM((2, C, T), BF16),
                pltpu.VMEM((STAGES, 3, NJ, 128), F32),
                pltpu.VMEM((STAGES, RING, 3, NJ, 128), F32),
                pltpu.VMEM((T, D), BF16),
                pltpu.VMEM((rows, 1, 128), F32),
                pltpu.VMEM((n_seq, 1, 128), F32),
                pltpu.VMEM((1, 128), F32),
                dma((5,)), dma((WSLOT,)), dma((STAGES,)), dma((STAGES,)),
                dma((STAGES, RING)), dma((STAGES, RING)), dma, dma, dma,
                dma((NT,)), dma((NT,)),
                dma, dma, dma, dma, dma,
            ],
            compiler_params=pltpu.CompilerParams(
                collective_id=0, has_side_effects=True, vmem_limit_bytes=46 * 1024 * 1024),
        )(*[
                pltpu.with_memory_space_constraint(v, pltpu.HBM)
                for v in (flat(cotangent), flat(conv_input), dec, angle.reshape(NJ, 128), flat(conv_weight), flat(in_weight))
            ])
        out, cm, tap = pl.pallas_call(
            finish,
            out_shape=(
                jax.ShapeDtypeStruct((T // 2, D), BF16),
                jax.ShapeDtypeStruct(cm.shape, BF16),
                jax.ShapeDtypeStruct(tap.shape, F32),
            ),
            in_specs=[V] * 4,
            out_specs=(HBM, HBM, HBM),
            scratch_shapes=[pltpu.VMEM((T // 2, D), BF16), dma((FIN + 3,))],
            compiler_params=pltpu.CompilerParams(vmem_limit_bytes=16 * 1024 * 1024),
        )(mine, part, cm, tap)
        tap = tap.reshape(4, NJ, 2, 128).transpose(0, 2, 1, 3).reshape(4, 2, C)
        return out, cm, tap

    in_specs = (
        P("seq", None, "ch"),
        P("seq", None, "ch"),
        P("seq", "ch"),
        P("ch"),
        P(None, None, "ch"),
        P(None, None, "ch"),
    )
    out_specs = (P(("seq", "ch"), None), P(None, ("ch", "seq"), None), P(None, None, "ch"))
    return jax.shard_map(on_device, mesh=mesh, in_specs=in_specs, out_specs=out_specs, check_vma=False)
```

```python
import functools

import jax
import jax.numpy as jnp
from jax import lax
from jax.experimental import pallas as pl
from jax.experimental.pallas import tpu as pltpu
from jax.sharding import PartitionSpec as P

MESH = pl.DeviceIdType.MESH
F32 = jnp.float32
BF16 = jnp.bfloat16
CHUNKS = 8
WCH = 2
WSLOT = 1
W1, W2, W3, W4 = 0, 1, 1, 2
H1, H2 = 2, 2
S2 = 6
PAD = 64
FIN = 4
NT = 8
RING = 4
STAGES = 3


def cmul(ar, ai, br, bi):
    return ar * br - ai * bi, ar * bi + ai * br


def scale_of(r):
    y = 0.25 * r
    q = y * (1.0 - y * (1 / 2) * (1.0 - y * (1 / 3) * (1.0 - y * (1 / 4) * (1.0 - y * (1 / 5) * (1.0 - y * (1 / 6))))))
    q = q * (2.0 - q)
    q = q * (2.0 - q)
    q = q * (2.0 - q)
    return jnp.sqrt(q)


def kernel(
    n_seq, T, C, D,
    cot_h, x_h, dec_h, ang_h, cw_h, w_h,
    mine_h, part_r, cm_h, tap_ref,
    ang_ref, cw_ref, cot_b, x_b, dec_b, w_b, halo,
    cot_f, x_f, e_f, sc_f, g_f, seed, sums, perm, wk, ftmp, feat, featT,
    mapv, maps, part, tbuf, trcv, trow,
    in_sem, w_sem, halo_s, halo_r, map_s, map_r, a2a_s, a2a_r, loc_s, par_s, par_r, t1_s, t1_r, t2_s, t2_r, o_sem,
):
    me = lax.axis_index("seq")
    ch = lax.axis_index("ch")
    other = 1 - ch
    NJ = C // 128
    L = T // CHUNKS
    strides = [RING**k for k in range(STAGES)]
    place = [lax.rem(me // st, RING) for st in strides]

    def ring(k, s):
        return me + (lax.rem(place[k] + s, RING) - place[k]) * strides[k]

    barrier = pltpu.get_barrier_semaphore()

    def greet(dev, core):
        pl.semaphore_signal(barrier, inc=1, device_id=(dev, core), device_id_type=MESH)

    for k in range(STAGES):
        for s in range(1, RING):
            greet(ring(k, s), ch)
    greet(me, other)
    greetings = STAGES * (RING - 1) + 1

    c_dec = pltpu.make_async_copy(dec_h, dec_b, in_sem.at[0])
    c_cot = pltpu.make_async_copy(cot_h, cot_b, in_sem.at[1])
    c_x = pltpu.make_async_copy(x_h, x_b, in_sem.at[2])
    c_ang = pltpu.make_async_copy(ang_h, ang_ref, in_sem.at[3])
    c_cw = pltpu.make_async_copy(cw_h, cw_ref, in_sem.at[4])
    c_dec.start()
    c_ang.start()
    c_cot.start()
    c_x.start()
    c_cw.start()
    wrows = w_h.shape[0] // WCH

    def w_copy(i):
        return pltpu.make_async_copy(
            w_h.at[pl.ds(i * wrows, wrows)], w_b.at[i % WSLOT], w_sem.at[i % WSLOT])

    for i in range(WSLOT):
        w_copy(i).start()


    def rowwise(src, dst, fn):
        def body(i, _):
            r = pl.multiple_of(i * 64, 64)
            dst[pl.ds(r, 64), :] = fn(src[pl.ds(r, 64), :].astype(F32))
            return 0

        lax.fori_loop(0, src.shape[0] // 64, body, 0)

    def pair(ref, t):
        return ref[pl.ds(2 * NJ * t, NJ, stride=2), :], ref[pl.ds(2 * NJ * t + 1, NJ, stride=2), :]

    c_dec.wait()
    rowwise(dec_b, e_f, lambda r: jnp.exp(-r))
    c_ang.wait()
    ang = ang_ref[...]
    cr = jnp.cos(ang)
    ci = -jnp.sin(ang)
    c_cot.wait()
    rowwise(cot_b, cot_f, lambda v: v)

    zero = jnp.zeros((NJ, 128), F32)
    one = jnp.ones((NJ, 128), F32)

    def at(t8, u):
        return pl.ds(8 * NJ * t8 + u, NJ, stride=8)

    def pass1(n, st):
        st = list(st)
        for u in reversed(range(8)):
            for c in range(CHUNKS):
                t8 = c * (L // 8) + L // 8 - 1 - n
                ur, ui, p = st[3 * c : 3 * c + 3]
                e = e_f[at(t8, u), :]
                a, b = pair(cot_f, t8 * 8 + u)
                ur, ui = cmul(e * cr, e * ci, a + ur, b + ui)
                st[3 * c : 3 * c + 3] = ur, ui, p * e
        return tuple(st)

    st = lax.fori_loop(0, L // 8, pass1, (zero, zero, one) * CHUNKS)

    def power(ar, ai, n):
        while n > 1:
            ar, ai = ar * ar - ai * ai, 2.0 * ar * ai
            n //= 2
        return ar, ai

    lr, li = power(cr, ci, L)
    rot = power(lr, li, CHUNKS)
    chunk_maps = []
    for c in range(CHUNKS):
        ur, ui, p = st[3 * c : 3 * c + 3]
        chunk_maps.append((p * lr, p * li, ur, ui))
    br, bi = zero, zero
    total = one
    for c in reversed(range(CHUNKS)):
        ar, ai, sr, si = chunk_maps[c]
        br, bi = cmul(ar, ai, br, bi)
        br, bi = br + sr, bi + si
        total = total * st[3 * c + 2]

    raw = dec_b[pl.ds(0, 8 * NJ), :].astype(F32)
    ftmp[0, pl.ds(0, 8 * NJ), :] = raw
    halo[0, pl.ds(0, 32), :] = cot_b[pl.ds(0, 32), :]
    firsts = [ftmp[0, pl.ds(t, NJ, stride=8), :] for t in range(3)]
    halo[0, pl.ds(32, 32), :] = jnp.concatenate(firsts + firsts[2:], 0).astype(BF16)
    pl.semaphore_wait(barrier, greetings)

    def halo_copy(k):
        return pltpu.make_async_remote_copy(
            src_ref=halo.at[k], dst_ref=halo.at[k + 1], send_sem=halo_s.at[k], recv_sem=halo_r.at[k],
            device_id=(ring(k, RING - 1), ch), device_id_type=MESH)

    edge = [None]
    for k in range(1, STAGES):
        top = place[k - 1] == RING - 1
        edge.append(top if k == 1 else jnp.logical_and(edge[-1], top))

    def passing(k, act):
        if k == 0:
            act(halo_copy(0))
        else:

            @pl.when(edge[k])
            def _():
                act(halo_copy(k))

    def map_copy(k, s):
        return pltpu.make_async_remote_copy(
            src_ref=mapv.at[k], dst_ref=maps.at[k, place[k]], send_sem=map_s.at[k, s], recv_sem=map_r.at[k, RING - s],
            device_id=(ring(k, s), ch), device_id_type=MESH)

    def send_map(k, p, br, bi):
        for i, v in enumerate((p, br, bi)):
            mapv[k, i] = v
            maps[k, place[k], i] = v
        for s in range(1, RING):
            map_copy(k, s).start()
        if k > 0:
            passing(k - 1, lambda c: c.wait_recv())
        passing(k, lambda c: c.start())

    def stage(k, rot):
        for s in range(1, RING):
            map_copy(k, s).wait_recv()
        ar, ai, br, bi, p = one, zero, zero, zero, one
        mine = None
        for j in reversed(range(RING)):
            here = place[k] == j
            now = (ar, ai, br, bi)
            mine = now if mine is None else tuple(jnp.where(here, x, y) for x, y in zip(now, mine))
            q = maps[k, j, 0]
            vr, vi = q * rot[0], q * rot[1]
            br, bi = cmul(vr, vi, br, bi)
            br, bi = br + maps[k, j, 1], bi + maps[k, j, 2]
            if j > 0:
                ar, ai = cmul(vr, vi, ar, ai)
            p = p * q
        return mine, (p, br, bi)

    send_map(0, total, br, bi)

    G = 32 * NJ
    r, c = (lax.broadcasted_iota(jnp.int32, (G, G), d) for d in range(2))
    plane, row = r // 16, r % 16
    perm[...] = (c == row * 2 * NJ + (plane % NJ) * 2 + plane // NJ).astype(F32).astype(BF16)

    def unpack_w(i):
        w_copy(i).wait()
        src = w_b.at[i % WSLOT]
        n = wrows // G
        x = jnp.concatenate([src[pl.ds(v * G, G), :] for v in range(n)], 1)
        y = jnp.dot(perm[...], x, preferred_element_type=F32).astype(BF16)
        for v in range(n):
            for q in range(2 * NJ):
                wk[q, pl.ds((i * n + v) * 16, 16), :] = y[q * 16 : q * 16 + 16, v * 128 : v * 128 + 128]
        if i + WSLOT < WCH:
            w_copy(i + WSLOT).start()

    rowwise(dec_b, sc_f, scale_of)
    c_x.wait()
    x_f[pl.ds(0, PAD), :] = jnp.zeros((PAD, 128), F32)

    def spread(i, _):
        r = pl.multiple_of(i * 64, 64)
        x_f[pl.ds(PAD + r, 64), :] = x_b[pl.ds(r, 64), :].astype(F32)
        return 0

    lax.fori_loop(0, x_b.shape[0] // 64, spread, 0)

    b, q = (zero, zero), (one, zero)
    for c in reversed(range(CHUNKS)):
        for i, v in enumerate(b + q):
            seed[c, i] = v
        ar, ai, sr, si = chunk_maps[c]
        b = cmul(ar, ai, *b)
        b = b[0] + sr, b[1] + si
        q = cmul(ar, ai, *q)
    for i in range(24):
        sums[i] = zero

    def split(lo, hi):
        def two(h, _):
            def body(n, st):
                st = list(st)
                xs = {}
                for u in reversed(range(8)):
                    for v in range(2):
                        t8 = (2 * h + v) * (L // 8) + L // 8 - 1 - n
                        t = t8 * 8 + u
                        br, bi, qr, qi = st[4 * v : 4 * v + 4]
                        a, b = pair(cot_f, t)
                        br, bi = a + br, b + bi
                        s = sc_f[at(t8, u), :]
                        vals = (s * br, s * bi, s * qr, s * qi)
                        for i, w in enumerate(vals):
                            g_f[t, i] = w
                        for k in range(4):
                            if (v, u - k) not in xs:
                                xs[v, u - k] = pair(x_f.at[pl.ds(pl.multiple_of(16 * t8 * NJ, 8), PAD + 16 * NJ)], u - k + PAD // (2 * NJ))
                            xr, xi = xs[v, u - k]
                            for i, w in enumerate((vals[0] * xr, vals[1] * xi, vals[2] * xr, vals[3] * xr, vals[2] * xi, vals[3] * xi)):
                                st[8 + 6 * k + i] = st[8 + 6 * k + i] + w
                        e = e_f[at(t8, u), :]
                        mr, mi = e * cr, e * ci
                        st[4 * v : 4 * v + 4] = (*cmul(mr, mi, br, bi), *cmul(mr, mi, qr, qi))
                return tuple(st)

            st = [seed[2 * h + v, i] for v in range(2) for i in range(4)]
            st = lax.fori_loop(0, L // 8, body, tuple(st + [sums[i] for i in range(24)]))
            for i in range(24):
                sums[i] = st[8 + i]
            return 0

        lax.fori_loop(lo, hi, two, 0)

    split(0, H1)
    for i in range(0, W1):
        unpack_w(i)

    later0, whole0 = stage(0, rot)
    send_map(1, *whole0)
    split(H1, H2)
    for i in range(W1, W2):
        unpack_w(i)
    rot1 = power(*rot, RING)
    later1, whole1 = stage(1, rot1)
    send_map(2, *whole1)
    split(H2, CHUNKS // 2)
    for i in range(W2, W3):
        unpack_w(i)
    later2, _ = stage(2, power(*rot1, RING))

    passing(STAGES - 1, lambda c: c.wait_recv())
    ur, ui = later2[2], later2[3]
    for ar, ai, br, bi in (later1, later0):
        ur, ui = cmul(ar, ai, ur, ui)
        ur, ui = ur + br, ui + bi

    last = me == n_seq - 1

    @pl.when(jnp.logical_not(last))
    def _():
        which = 1 + jnp.where(edge[1], 1, 0) + jnp.where(edge[2], 1, 0)
        rows = halo[which].astype(F32)
        ftmp[0, pl.ds(0, 64), :] = rows
        vr, vi = ur, ui
        for t in range(3):
            r = rows[32 + t * NJ : 32 + (t + 1) * NJ, :]
            e = jnp.exp(r)
            vr, vi = cmul(e * cr, -e * ci, vr, vi)
            s = scale_of(r)
            g_f[T + t, 0] = s * vr
            g_f[T + t, 1] = s * vi
            g_f[T + t, 2] = zero
            g_f[T + t, 3] = zero
            if t < 2:
                a, b = pair(ftmp.at[0], t)
                vr, vi = vr - a, vi - b

    @pl.when(last)
    def _():
        for t in range(3):
            for i in range(4):
                g_f[T + t, i] = zero

    for k in range(4):
        a = [sums[6 * k + i] for i in range(6)]
        acc = [a[0] + a[2] * ur - a[3] * ui, a[1] + a[4] * ui + a[5] * ur]
        for t in range(k):
            x = pair(x_f, T + t - k + PAD // (2 * NJ))
            for p in range(2):
                acc[p] = acc[p] + g_f[T + t, p] * x[p]
        for p in range(2):
            for jt in range(NJ):
                tbuf[2 * NJ * k + 2 * jt + p] = acc[p][jt : jt + 1, :]
    trcv[me] = tbuf[me]

    def t1(dst_dev):
        return pltpu.make_async_remote_copy(
            src_ref=tbuf.at[dst_dev], dst_ref=trcv.at[me], send_sem=t1_s, recv_sem=t1_r,
            device_id=(dst_dev, ch), device_id_type=MESH)

    def t2(dst_dev):
        return pltpu.make_async_remote_copy(
            src_ref=trow, dst_ref=tap_ref.at[me], send_sem=t2_s, recv_sem=t2_r,
            device_id=(dst_dev, ch), device_id_type=MESH)

    def others(fn):
        def body(s, _):
            j = me + s
            fn(jnp.where(j >= n_seq, j - n_seq, j))
            return 0

        lax.fori_loop(1, n_seq, body, 0)

    others(lambda j: t1(j).start())

    c_cw.wait()
    cw = [[cw_ref[pl.ds(2 * NJ * k + p, NJ, stride=2), :] for p in range(2)] for k in range(4)]

    def conv(i, _):
        def full(t):
            hr, hi = cmul(g_f[t, 2], g_f[t, 3], ur, ui)
            return g_f[t, 0] + hr, g_f[t, 1] + hi

        both = [full(i * 16 + k) for k in range(19)]
        for p in range(2):
            g = [v[p] for v in both]
            for u in range(16):
                f = cw[0][p] * g[u] + cw[1][p] * g[u + 1] + cw[2][p] * g[u + 2] + cw[3][p] * g[u + 3]
                ftmp[p, pl.ds((u // 8) * 8 * NJ + u % 8, NJ, stride=8), :] = f
            for jt in range(NJ):
                v = jnp.concatenate([ftmp[p, pl.ds(jt * 8, 8), :], ftmp[p, pl.ds(8 * NJ + jt * 8, 8), :]], 0)
                feat[p * NJ + jt, pl.ds(pl.multiple_of(i * 16, 16), 16), :] = v.astype(BF16)
        return 0

    lax.fori_loop(0, T // 16, conv, 0)

    own = C // n_seq
    per = 128 // own

    def a2a_src(dst_dev):
        return featT.at[:, pl.ds(pl.multiple_of(dst_dev * own, own), own), :]

    cm_mine = cm_h.at[:, :, pl.ds(pl.multiple_of(me * T, T), T)]

    def a2a_copy(dst_dev):
        return pltpu.make_async_remote_copy(
            src_ref=a2a_src(dst_dev), dst_ref=cm_mine, send_sem=a2a_s, recv_sem=a2a_r,
            device_id=(dst_dev, ch), device_id_type=MESH)

    local = pltpu.make_async_copy(a2a_src(me), cm_mine, loc_s)

    def turn(s, _):
        jt = me // per + s
        jt = jnp.where(jt >= NJ, jt - NJ, jt)
        for p in range(2):
            featT[p, pl.ds(pl.multiple_of(jt * 128, 128), 128), :] = feat[p * NJ + jt].T
        for q in range(per):
            j = jt * per + q

            @pl.when(j != me)
            def _():
                a2a_copy(j).start()

        return 0

    lax.fori_loop(0, S2, turn, 0)

    for i in range(W3, W4):
        unpack_w(i)

    def all_but_one(ref, sem):
        part_of = ref.at[pl.ds(0, n_seq - 1)]
        return pltpu.make_async_copy(part_of, part_of, sem)

    all_but_one(trcv, t1_r).wait()
    row = jnp.sum(trcv[...], axis=0)
    trow[...] = row
    tap_ref[me] = row
    others(lambda j: t2(j).start())

    for i in range(W4, WCH):
        unpack_w(i)

    lax.fori_loop(S2, NJ, turn, 0)
    local.start()

    nt = D // NT
    half = T // 2

    def par_copy(n):
        cols = pl.ds(pl.multiple_of(n * nt, nt), nt)
        return pltpu.make_async_remote_copy(
            src_ref=part.at[pl.ds(pl.multiple_of(other * half, half), half), cols], dst_ref=part_r.at[:, cols],
            send_sem=par_s.at[n], recv_sem=par_r.at[n], device_id=(me, other), device_id_type=MESH)

    def mine_copy(n):
        cols = pl.ds(pl.multiple_of(n * nt, nt), nt)
        return pltpu.make_async_copy(
            part.at[pl.ds(pl.multiple_of(ch * half, half), half), cols], mine_h.at[:, cols], o_sem.at[n])

    def tile(n, _):
        rows = pl.ds(pl.multiple_of(n * nt, nt), nt)
        lhs = jnp.concatenate([feat[i] for i in range(2 * NJ)], 1)
        rhs = jnp.concatenate([wk[i, rows, :] for i in range(2 * NJ)], 1)
        y = lax.dot_general(lhs, rhs, (((1,), (1,)), ((), ())), preferred_element_type=F32)
        part[:, rows] = y.astype(BF16)
        par_copy(n).start()
        mine_copy(n).start()
        return 0

    lax.fori_loop(0, NT, tile, 0)


    for k in range(STAGES):
        for s in range(1, RING):
            map_copy(k, s).wait_send()

    for k in range(STAGES):
        passing(k, lambda c: c.wait_send())

    def ends(n, _):
        par_copy(n).wait()
        mine_copy(n).wait()
        return 0

    lax.fori_loop(0, NT, ends, 0)
    all_but_one(trcv, t1_s).wait()
    all_but_one(trcv, t2_s).wait()
    all_but_one(tap_ref, t2_r).wait()
    local.wait()
    sent = featT.at[:, pl.ds(0, C - own), :]
    pltpu.make_async_copy(sent, sent, a2a_s).wait()
    came = cm_h.at[:, :, pl.ds(0, T * (n_seq - 1))]
    pltpu.make_async_copy(came, came, a2a_r).wait()


def finish(mine, part, cm, tap, out_h, cm_h, tap_h, out, sem):
    rows = mine.shape[0] // FIN
    copies = [pltpu.make_async_copy(cm.at[p], cm_h.at[p], sem.at[FIN + p]) for p in range(2)]
    copies.append(pltpu.make_async_copy(tap, tap_h, sem.at[FIN + 2]))
    for c in copies:
        c.start()
    for i in range(FIN):
        r = pl.ds(i * rows, rows)
        out[r, :] = (mine[r, :].astype(F32) + part[r, :].astype(F32)).astype(BF16)
        copies.append(pltpu.make_async_copy(out.at[r], out_h.at[r], sem.at[i]))
        copies[-1].start()
    for c in copies:
        c.wait()


def solution(mesh):
    n_seq = mesh.shape["seq"]

    def flat(a):
        lead = a.shape[0]
        return a.reshape(lead, 2, -1, 128).transpose(0, 2, 1, 3).reshape(-1, 128)

    def on_device(cotangent, conv_input, decay_rate, angle, conv_weight, in_weight):
        T, _, C = cotangent.shape
        D = in_weight.shape[0]
        NJ = C // 128
        dec = decay_rate.reshape(T // 8, 8, NJ, 128).transpose(0, 2, 1, 3).reshape(-1, 128)
        dma = pltpu.SemaphoreType.DMA
        ANY = pl.BlockSpec(memory_space=pl.ANY)
        V = pl.BlockSpec(memory_space=pltpu.VMEM)
        rows = 8 * NJ
        HBM = pl.BlockSpec(memory_space=pltpu.HBM)
        mine, part, cm, tap = pl.pallas_call(
            functools.partial(kernel, n_seq, T, C, D),
            out_shape=(
                jax.ShapeDtypeStruct((T // 2, D), BF16),
                jax.ShapeDtypeStruct((T // 2, D), BF16),
                jax.ShapeDtypeStruct((2, C // n_seq, T * n_seq), BF16),
                jax.ShapeDtypeStruct((rows, 1, 128), F32),
            ),
            in_specs=[HBM] * 6,
            out_specs=(ANY, ANY, ANY, V),
            scratch_shapes=[
                pltpu.VMEM((NJ, 128), F32),
                pltpu.VMEM((8 * NJ, 128), F32),
                pltpu.VMEM((T * 2 * NJ, 128), BF16),
                pltpu.VMEM((T * 2 * NJ, 128), BF16),
                pltpu.VMEM((T * NJ, 128), BF16),
                pltpu.VMEM((WSLOT, D * 2 * NJ // WCH, 128), BF16),
                pltpu.VMEM((STAGES + 1, 64, 128), BF16),
                pltpu.VMEM((T * 2 * NJ, 128), F32),
                pltpu.VMEM((T * 2 * NJ + PAD, 128), F32),
                pltpu.VMEM((T * NJ, 128), F32),
                pltpu.VMEM((T * NJ, 128), F32),
                pltpu.VMEM((T + 3, 4, NJ, 128), F32),
                pltpu.VMEM((CHUNKS, 4, NJ, 128), F32),
                pltpu.VMEM((24, NJ, 128), F32),
                pltpu.VMEM((32 * NJ, 32 * NJ), BF16),
                pltpu.VMEM((2 * NJ, D, 128), BF16),
                pltpu.VMEM((2, 16 * NJ, 128), F32),
                pltpu.VMEM((2 * NJ, T, 128), BF16),
                pltpu.VMEM((2, C, T), BF16),
                pltpu.VMEM((STAGES, 3, NJ, 128), F32),
                pltpu.VMEM((STAGES, RING, 3, NJ, 128), F32),
                pltpu.VMEM((T, D), BF16),
                pltpu.VMEM((rows, 1, 128), F32),
                pltpu.VMEM((n_seq, 1, 128), F32),
                pltpu.VMEM((1, 128), F32),
                dma((5,)), dma((WSLOT,)), dma((STAGES,)), dma((STAGES,)),
                dma((STAGES, RING)), dma((STAGES, RING)), dma, dma, dma,
                dma((NT,)), dma((NT,)),
                dma, dma, dma, dma, dma((NT,)),
            ],
            compiler_params=pltpu.CompilerParams(
                collective_id=0, has_side_effects=True, vmem_limit_bytes=46 * 1024 * 1024),
        )(*[
                pltpu.with_memory_space_constraint(v, pltpu.HBM)
                for v in (flat(cotangent), flat(conv_input), dec, angle.reshape(NJ, 128), flat(conv_weight), flat(in_weight))
            ])
        out, cm, tap = pl.pallas_call(
            finish,
            out_shape=(
                jax.ShapeDtypeStruct((T // 2, D), BF16),
                jax.ShapeDtypeStruct(cm.shape, BF16),
                jax.ShapeDtypeStruct(tap.shape, F32),
            ),
            in_specs=[V] * 4,
            out_specs=(HBM, HBM, HBM),
            scratch_shapes=[pltpu.VMEM((T // 2, D), BF16), dma((FIN + 3,))],
            compiler_params=pltpu.CompilerParams(vmem_limit_bytes=16 * 1024 * 1024),
        )(mine, part, cm, tap)
        tap = tap.reshape(4, NJ, 2, 128).transpose(0, 2, 1, 3).reshape(4, 2, C)
        return out, cm, tap

    in_specs = (
        P("seq", None, "ch"),
        P("seq", None, "ch"),
        P("seq", "ch"),
        P("ch"),
        P(None, None, "ch"),
        P(None, None, "ch"),
    )
    out_specs = (P(("seq", "ch"), None), P(None, ("ch", "seq"), None), P(None, None, "ch"))
    return jax.shard_map(on_device, mesh=mesh, in_specs=in_specs, out_specs=out_specs, check_vma=False)
```
